32 devices in a mesh: fam: 2 (over x), tm: 8 (over z, y), chan: 2 (over core).
Axes of the slice: x: 2, y: 2, z: 4, core: 2. Of those that a mesh axis runs over, the one named last changes fastest.
Arguments:
- records: float32 [3072, 4096], P(('fam', 'tm', 'chan')), parts along dimension 0, may hold values from -6 to 6
- row_dest: int32 [3072], P(('fam', 'tm', 'chan')), parts along dimension 0, may hold values from -1 to 7, as said below
- row_chan: int32 [3072], P(('fam', 'tm', 'chan')), parts along dimension 0, may hold values from 0 to 47, as said below
- row_len: int32 [3072], P(('fam', 'tm', 'chan')), parts along dimension 0, may hold values from 2048 to 4096
- templates: float32 [64, 16, 256], P(('fam', 'tm'), 'chan'), parts along dimension 0, may hold values from -6 to 6
- tmpl_chan: int32 [64, 16], P(('fam', 'tm'), 'chan'), parts along dimension 0, may hold values from 0 to 47
- tmpl_off: int32 [64, 16], P(('fam', 'tm'), 'chan'), parts along dimension 0, may hold values from 0 to 255
Outputs:
- detection: float32 [16, 4, 4, 3584], P(('fam', 'tm'), None, None, 'chan'), parts along dimension 0
The draws below stay inside these ranges and needn't reach their ends.
There are 2 independent parts, one for each index of `fam`. The reference program is written for one: setup_inputs(seed, part) draws one part's arguments, and reference() takes and returns one part's arrays. A program takes and returns all parts, laid end to end along the dimension named above; each array names one. Nothing has to cross between parts.
Inputs may be any that keep to these rules, and one draw needn't show every extreme that they name: `row_dest`: within the slots of the owners in one channel half, every pair of a time segment and a channel appears exactly once; one owner holds at most 12 rows of one time segment, and some owner holds exactly 12 of each. `row_chan`: 0 on empty slots.
All inputs are finite; a program needn't handle non-finite values.
Results may differ from the reference program's by a relative error of at most 0.0003.
Values sent between devices are 32-bit elements; how exact they have to be, the bound alone decides.
No kernel may reach another device: no remote copies, remote signals or barrier semaphores. Data moves between devices by JAX's collectives and lax.ppermute only.
A program may use at most 128 MiB of HBM per device.

```python
import jax
import jax.numpy as jnp
from jax import lax

SAMPLES = 4096
TLEN = 256
TCH = 16
MAXOFF = 256
STOPS = 4
CH_DEV = 48
SLOTS = 96
OWN_ROWS = 1536
NT_DEV = 4
NTEMPL = 32
LAGS = 3584
N_TM = 8
N_CHAN = 2


def routing_tables(key):
    capacity = 2 * CH_DEV // N_TM
    busy_count = N_TM // 4
    busy_slots = busy_count * capacity
    spare_count = CH_DEV - busy_slots

    def one_half(half_key):
        order = jax.random.permutation(jax.random.fold_in(half_key, 1), N_TM)
        ranking = jnp.argsort(order)

        def one_segment(segment_key):
            channels = jax.random.permutation(jax.random.fold_in(segment_key, 1), CH_DEV).astype(jnp.int32)
            picks = jax.random.permutation(jax.random.fold_in(segment_key, 2), (N_TM - busy_count) * capacity)[:spare_count]
            table = jnp.full((N_TM * capacity,), -1, jnp.int32)
            table = table.at[jnp.arange(busy_slots)].set(channels[:busy_slots])
            table = table.at[busy_slots + picks].set(channels[busy_slots:])
            return table.reshape(N_TM, capacity)[ranking]
        segment_keys = jax.vmap(lambda number: jax.random.fold_in(half_key, number + 7))(jnp.arange(N_TM))
        return jax.vmap(one_segment)(segment_keys)
    half_keys = jax.vmap(lambda number: jax.random.fold_in(key, number + 101))(jnp.arange(N_CHAN))
    tables = jax.vmap(one_half)(half_keys)
    tables = jnp.transpose(tables, (2, 0, 1, 3)).reshape(N_TM * N_CHAN, 2 * CH_DEV)
    segment_ids = jnp.broadcast_to(jnp.arange(N_TM, dtype=jnp.int32)[:, None], (N_TM, capacity)).reshape(-1)
    dest_rows = jnp.where(tables >= 0, segment_ids[None, :], -1)
    shuffle_keys = jax.vmap(lambda number: jax.random.fold_in(key, number + 5003))(jnp.arange(N_TM * N_CHAN))
    shuffles = jax.vmap(lambda shuffle_key: jax.random.permutation(shuffle_key, 2 * CH_DEV))(shuffle_keys)
    chan_rows = jnp.take_along_axis(tables, shuffles, axis=1)
    dest_rows = jnp.take_along_axis(dest_rows, shuffles, axis=1)
    return (dest_rows.reshape(-1).astype(jnp.int32), jnp.maximum(chan_rows, 0).reshape(-1).astype(jnp.int32))


def draw_row_dest(key, part):
    return routing_tables(key)[0]


def draw_row_chan(key, part):
    return routing_tables(key)[1]


def draw_row_len(key, part):
    lengths = jax.random.randint(jax.random.fold_in(key, 31), (OWN_ROWS,), SAMPLES // 2, SAMPLES + 1)
    full_spot = jax.random.randint(jax.random.fold_in(key, 32), (), 0, OWN_ROWS)
    return lengths.at[full_spot].set(SAMPLES).astype(jnp.int32)


def place_ends(entries, rng, low, largest):
    index_at = [jax.random.randint(jax.random.fold_in(rng, axis), (), 0, length) for axis, length in enumerate(entries.shape)]
    widest = entries.shape.index(max(entries.shape))
    next_to = index_at[:widest] + [(index_at[widest] + 1) % entries.shape[widest]] + index_at[widest + 1:]
    return entries.at[tuple(index_at)].set(low).at[tuple(next_to)].set(largest)


def block_scale(rng, shape, shards, least, largest):
    def one(position, shards_of):
        heights = jax.random.uniform(jax.random.fold_in(jax.random.fold_in(rng, 6), position), (shards_of,), jnp.float32, least / len(shards), largest / len(shards))
        return jnp.repeat(jnp.exp(heights), shape[position] // shards_of).reshape((-1,) + (1,) * (len(shape) - position - 1))

    factor_of = one(*shards[0])
    for cut in shards[1:]:
        factor_of = factor_of * one(*cut)
    return factor_of


def gaussian(key, extent, deviation, reach, shards=(), held_as=jnp.bfloat16):
    result = deviation * jax.random.normal(key, extent, jnp.float32)
    if shards:
        result = result * block_scale(key, extent, shards, -0.22, 0.18)
    return jnp.clip(result, -reach, reach).astype(held_as)


def setup_inputs(seed: int = 0, part: int = 0) -> dict:
    arg_keys = jax.random.split(jax.random.key(seed), 8)
    part_splits = jax.random.split(jax.random.fold_in(arg_keys[7], part), 8)
    return {
        "records": gaussian(part_splits[0], (OWN_ROWS, SAMPLES), 1.0, 6.0, ((0, 16),), jnp.float32),
        "row_dest": draw_row_dest(jax.random.fold_in(jax.random.fold_in(arg_keys[7], part), 71), part),
        "row_chan": draw_row_chan(jax.random.fold_in(jax.random.fold_in(arg_keys[7], part), 71), part),
        "row_len": draw_row_len(jax.random.fold_in(jax.random.fold_in(arg_keys[7], part), 71), part),
        "templates": gaussian(part_splits[4], (NTEMPL, TCH, TLEN), 1.0, 6.0, ((0, 8), (1, 2)), jnp.float32),
        "tmpl_chan": place_ends(jax.random.randint(part_splits[5], (NTEMPL, TCH), 0, CH_DEV), jax.random.fold_in(part_splits[5], 1), 0, CH_DEV - 1).astype(jnp.int32),
        "tmpl_off": place_ends(jax.random.randint(part_splits[6], (NTEMPL, TCH), 0, MAXOFF), jax.random.fold_in(part_splits[6], 1), 0, MAXOFF - 1).astype(jnp.int32),
    }


FLOOR_SHARE = 0.25
TEMPLATE_EPS = 1e-06

def normalized(template_rows):
    centred = template_rows - lax.optimization_barrier(jnp.mean(template_rows, axis=-1, keepdims=True))
    energy = lax.optimization_barrier(jnp.sum(centred * centred, axis=-1, keepdims=True))
    return centred / jnp.sqrt(energy + TLEN * TEMPLATE_EPS)

def reference(records, row_dest, row_chan, row_len, templates, tmpl_chan, tmpl_off):
    positions = jnp.arange(SAMPLES, dtype=jnp.int32)
    masked = jnp.where(positions[None, :] < row_len[:, None], records, jnp.zeros_like(records))
    owner_half = (jnp.arange(OWN_ROWS, dtype=jnp.int32) // SLOTS % N_CHAN).astype(jnp.int32)
    target = jnp.where(row_dest >= 0, row_dest, N_TM).astype(jnp.int32)
    waveform = jnp.zeros((N_TM + 1, N_CHAN, CH_DEV, SAMPLES), records.dtype)
    waveform = waveform.at[target, owner_half, row_chan.astype(jnp.int32)].set(masked)[:N_TM]
    span_count = SAMPLES - TLEN
    zero_col = jnp.zeros(waveform.shape[:-1] + (1,), waveform.dtype)
    run_sum = jnp.concatenate([zero_col, jnp.cumsum(waveform, axis=-1)], axis=-1)
    run_sq = jnp.concatenate([zero_col, jnp.cumsum(waveform * waveform, axis=-1)], axis=-1)
    win_sum = run_sum[..., TLEN:TLEN + span_count] - run_sum[..., :span_count]
    win_sq = run_sq[..., TLEN:TLEN + span_count] - run_sq[..., :span_count]
    variance = win_sq - win_sum * win_sum / TLEN
    inv_sigma = 1.0 / jnp.sqrt(jnp.maximum(variance, FLOOR_SHARE * TLEN))
    spectra = jnp.fft.rfft(waveform, axis=-1)
    unit = normalized(templates)
    unit_spec = jnp.conj(jnp.fft.rfft(unit, n=SAMPLES, axis=-1))
    per_half = TCH // N_CHAN
    half_of = (jnp.arange(TCH, dtype=jnp.int32) // per_half).astype(jnp.int32)
    stack_gain = jnp.sqrt(1.0 * TLEN * TCH) / TCH

    def window_cut(row_corr, row_scale, offset):
        first = lax.dynamic_slice_in_dim(row_corr, offset, LAGS)
        second = lax.dynamic_slice_in_dim(row_scale, offset, LAGS)
        return first * second

    def one_segment(segment_index):
        segment_spec = spectra[segment_index]
        segment_scale = inv_sigma[segment_index]
        results = []
        for stop_index in range(STOPS):
            anchor = ((segment_index - stop_index) % N_TM).astype(jnp.int32)
            block_spec = lax.dynamic_slice_in_dim(unit_spec, anchor * NT_DEV, NT_DEV, 0)
            block_chan = lax.dynamic_slice_in_dim(tmpl_chan, anchor * NT_DEV, NT_DEV, 0)
            block_off = lax.dynamic_slice_in_dim(tmpl_off, anchor * NT_DEV, NT_DEV, 0)
            data_spec = segment_spec[half_of[None, :], block_chan]
            full_corr = jnp.fft.irfft(block_spec * data_spec, n=SAMPLES, axis=-1)
            scales = segment_scale[half_of[None, :], block_chan]
            ratios = jax.vmap(jax.vmap(window_cut))(full_corr, scales, block_off)
            results.append(stack_gain * lax.optimization_barrier(jnp.sum(ratios, axis=1)))
        return jnp.stack(results)
    return lax.map(one_segment, jnp.arange(N_TM, dtype=jnp.int32))
```

```python
import functools

import jax
import jax.numpy as jnp
from jax import lax
from jax.experimental import pallas as pl
from jax.experimental.pallas import tpu as pltpu
from jax.sharding import PartitionSpec as P

TCH = 16
MAXOFF = 256
STOPS = 4
LANES = 128
UNROLL = 4

FLOOR_SHARE = 0.25
TEMPLATE_EPS = 1e-06


def normalized(template_rows):
    centred = template_rows - jnp.mean(template_rows, axis=-1, keepdims=True)
    energy = jnp.sum(centred * centred, axis=-1, keepdims=True)
    return centred / jnp.sqrt(energy + template_rows.shape[-1] * TEMPLATE_EPS)


def pack_kernel(half, capacity, dest, chan, length, where, rec, out, count, source):
    slot_count = dest.shape[0]
    blocks = rec.shape[1]
    member = where[0]

    def clear_count(i, c):
        count[i] = 0
        return c

    lax.fori_loop(0, count.shape[0], clear_count, 0)

    def clear_source(i, c):
        source[i] = -1
        return c

    lax.fori_loop(0, slot_count, clear_source, 0, unroll=8)

    def place(r, c):
        d = dest[r]
        used = d >= 0
        d = jnp.where(used, d, 2 * half)
        step = jnp.bitwise_xor(lax.rem(d, half), member)
        side = lax.div(d, half)
        rank = count[d]
        count[d] = rank + 1
        pos = (step * 2 + side) * capacity + rank
        source[jnp.where(used, pos, slot_count)] = r
        return c

    lax.fori_loop(0, slot_count, place, 0, unroll=4)
    flat = lax.broadcasted_iota(jnp.int32, (blocks, LANES), 0) * LANES + lax.broadcasted_iota(
        jnp.int32, (blocks, LANES), 1
    )
    last = blocks * LANES - 1

    def emit(pos, c):
        r = source[pos]
        used = r >= 0
        row = jnp.maximum(r, 0)
        limit = jnp.where(used, length[row], 0)
        tag = jnp.where(used, chan[row], -1).astype(jnp.float32)
        tile = jnp.where(flat < limit, rec[row], 0.0)
        out[pos] = jnp.where(flat == last, tag, tile)
        return c

    lax.fori_loop(0, slot_count, emit, 0, unroll=2)


def pack_rows(records, row_dest, row_chan, row_len, where, half):
    slot_count, sample_count = records.shape
    capacity = slot_count // (2 * half)
    smem = pl.BlockSpec(memory_space=pltpu.SMEM)
    vmem = pl.BlockSpec(memory_space=pltpu.VMEM)
    return pl.pallas_call(
        functools.partial(pack_kernel, half, capacity),
        out_shape=jax.ShapeDtypeStruct((slot_count, sample_count // LANES, LANES), jnp.float32),
        in_specs=[smem, smem, smem, smem, vmem],
        out_specs=vmem,
        scratch_shapes=[
            pltpu.SMEM((2 * half + 1,), jnp.int32),
            pltpu.SMEM((slot_count + 1,), jnp.int32),
        ],
        name="pack_rows",
    )(row_dest, row_chan, row_len, where, records.reshape(slot_count, -1, LANES))


def split(x):
    high = x.astype(jnp.bfloat16)
    return high, (x - high.astype(jnp.float32)).astype(jnp.bfloat16)


def segment_kernel(shape, tags, chans, offs, where, *refs):
    parts, capacity, blocks, taps, per_block, half_taps, lags = shape
    rows_in = refs[:parts]
    templ_in = refs[parts : parts + STOPS]
    keep, send = refs[parts + STOPS : parts + STOPS + 2]
    x_sc, s_sc, q_sc, inv_sc, h_sc, u_sc, acc, table, pair_id, pair_slot = refs[parts + STOPS + 2 :]
    side = where[0]
    core = where[1]
    slot_count = parts * capacity
    rows = slot_count * blocks
    stack_count = STOPS * per_block
    pair_count = stack_count * half_taps
    channel_count = table.shape[0] - 1
    stack_gain = (taps * TCH) ** 0.5 / TCH

    def clear(i, c):
        table[i] = -1
        return c

    lax.fori_loop(0, channel_count, clear, 0, unroll=8)

    def mark(i, c):
        tag = tags[side, i]
        table[jnp.where(tag >= 0, tag, channel_count)] = i
        return c

    lax.fori_loop(0, slot_count, mark, 0, unroll=4)

    def gather_pairs(i, filled):
        slot = table[chans[i]]
        pair_id[filled] = i
        pair_slot[filled] = slot
        return filled + jnp.where(slot >= 0, 1, 0)

    found = lax.fori_loop(0, pair_count, gather_pairs, 0, unroll=4)
    groups = lax.div(found + UNROLL - 1, UNROLL)

    def fill(i, c):
        pair_id[found + i] = stack_count * half_taps
        pair_slot[found + i] = 0
        return c

    lax.fori_loop(0, UNROLL, fill, 0)

    for s in range(STOPS):
        u_sc[s * per_block * half_taps * 2 : (s + 1) * per_block * half_taps * 2, :] = templ_in[s][
            : per_block * half_taps * 2, :
        ]
    u_sc[pair_count * 2 :, :] = jnp.zeros((8, LANES), jnp.float32)
    acc[...] = jnp.zeros_like(acc)
    part_rows = capacity * blocks
    for k in range(parts):
        x_sc[k * part_rows : (k + 1) * part_rows, :] = rows_in[k][side].reshape(part_rows, LANES)
    x_sc[rows:, :] = jnp.zeros((8, LANES), jnp.float32)

    row_i = lax.broadcasted_iota(jnp.int32, (LANES, LANES), 0)
    lane_i = lax.broadcasted_iota(jnp.int32, (LANES, LANES), 1)
    lower = row_i >= lane_i
    tail = lower.astype(jnp.float32).astype(jnp.bfloat16)
    ones = jnp.ones((LANES, LANES), jnp.bfloat16)
    sums = jnp.concatenate([tail, ones], axis=1)
    sums = jnp.concatenate([sums, sums], axis=0)
    chunk_slots = 8 if slot_count % 8 == 0 else 1
    chunk = chunk_slots * blocks

    def prepare(g, c):
        base = pl.multiple_of(g * chunk, chunk)
        x0 = x_sc[pl.ds(base, chunk), :]
        high0, low0 = split(x0)
        s_sc[:chunk, :] = jnp.dot(
            jnp.concatenate([high0, low0], axis=1), sums, preferred_element_type=jnp.float32
        )
        square_high, square_low = split(x0 * x0)
        q_sc[:chunk, :] = jnp.dot(
            jnp.concatenate([square_high, square_low], axis=1),
            sums,
            preferred_element_type=jnp.float32,
        )

        def window(ref):
            return (
                ref[:chunk, :LANES]
                + ref[pl.ds(1, chunk), LANES:]
                + (ref[pl.ds(2, chunk), LANES:] - ref[pl.ds(2, chunk), :LANES])
            )

        win_sum = window(s_sc)
        variance = window(q_sc) - win_sum * win_sum / taps
        inv = stack_gain / jnp.sqrt(jnp.maximum(variance, FLOOR_SHARE * taps))
        inv_sc[pl.ds(base, chunk), :] = inv
        high1, low1 = split(x_sc[pl.ds(base + 1, chunk), :])
        high2, low2 = split(x_sc[pl.ds(base + 2, chunk), :])
        slot0 = g * chunk_slots
        for j, (high, low) in enumerate(((high0, low0), (high1, low1), (high2, low2))):
            lanes = slice(j * LANES, (j + 1) * LANES)
            h_sc[pl.ds(slot0, chunk_slots), :blocks, lanes] = high.reshape(
                chunk_slots, blocks, LANES
            )
            h_sc[pl.ds(slot0, chunk_slots), blocks:, lanes] = low.reshape(
                chunk_slots, blocks, LANES
            )
        return c

    s_sc[chunk:, :] = jnp.zeros((8, 2 * LANES), jnp.float32)
    q_sc[chunk:, :] = jnp.zeros((8, 2 * LANES), jnp.float32)
    lax.fori_loop(0, slot_count // chunk_slots, prepare, 0)

    lane_b = lax.broadcasted_iota(jnp.int32, (blocks, LANES), 1)

    def circulant(row):
        return pltpu.roll(
            jnp.broadcast_to(u_sc[pl.ds(row, 1), :], (LANES, LANES)), 0, 1, stride=1, stride_axis=0
        )

    def pairs(g, c):
        for j in range(UNROLL):
            pair = pair_id[g * UNROLL + j]
            slot = pair_slot[g * UNROLL + j]
            first = circulant(pair * 2)
            second = circulant(pair * 2 + 1)
            zero = jnp.zeros_like(first)
            bands = []
            for band in (
                jnp.where(lower, first, zero),
                jnp.where(lower, second, first),
                jnp.where(lower, zero, second),
            ):
                bands.append(jnp.concatenate(split(band), axis=1))
            weights = jnp.concatenate(bands, axis=0)
            terms = jnp.dot(h_sc[slot], weights, preferred_element_type=jnp.float32)
            corr = (terms[:blocks, :LANES] + terms[:blocks, LANES:]) + (
                terms[blocks:, :LANES] + terms[blocks:, LANES:]
            )
            ratio = corr * inv_sc[pl.ds(pl.multiple_of(slot * blocks, blocks), blocks), :]
            off = offs[pair]
            by_lane = lax.rem(off, LANES)
            whole = off >= LANES
            here = pltpu.roll(ratio, lax.rem(LANES - by_lane, LANES), 1)
            after = pltpu.roll(here, blocks - 1, 0)
            beyond = pltpu.roll(here, blocks - 2, 0)
            moved = jnp.where(
                lane_b < LANES - by_lane,
                jnp.where(whole, after, here),
                jnp.where(whole, beyond, after),
            )
            stack = lax.div(pair, half_taps)
            acc[stack] += moved
        return c

    lax.fori_loop(0, groups, pairs, 0)

    half_lags = lags // 2 // LANES
    for which, ref in ((core, keep), (1 - core, send)):
        for b in range(half_lags):
            ref[:, b * LANES : (b + 1) * LANES] = jnp.where(
                which == 0, acc[:stack_count, b, :], acc[:stack_count, half_lags + b, :]
            )


def segment_stack(rows, templates, tags, chans, offs, where, shape):
    parts, capacity, blocks, taps, per_block, half_taps, lags = shape
    slot_count = parts * capacity
    stack_count = STOPS * per_block
    pair_count = stack_count * half_taps
    chunk = (8 if slot_count % 8 == 0 else 1) * blocks
    smem = pl.BlockSpec(memory_space=pltpu.SMEM)
    vmem = pl.BlockSpec(memory_space=pltpu.VMEM)
    out = jax.ShapeDtypeStruct((stack_count, lags // 2), jnp.float32)
    return pl.pallas_call(
        functools.partial(segment_kernel, shape),
        out_shape=(out, out),
        in_specs=[smem] * 4 + [vmem] * (parts + STOPS),
        out_specs=(vmem, vmem),
        scratch_shapes=[
            pltpu.VMEM((slot_count * blocks + 8, LANES), jnp.float32),
            pltpu.VMEM((chunk + 8, 2 * LANES), jnp.float32),
            pltpu.VMEM((chunk + 8, 2 * LANES), jnp.float32),
            pltpu.VMEM((slot_count * blocks, LANES), jnp.float32),
            pltpu.VMEM((slot_count, 2 * blocks, 3 * LANES), jnp.bfloat16),
            pltpu.VMEM((pair_count * 2 + 8, LANES), jnp.float32),
            pltpu.VMEM((stack_count + 1, blocks, LANES), jnp.float32),
            pltpu.SMEM((slot_count + 1,), jnp.int32),
            pltpu.SMEM((pair_count + UNROLL,), jnp.int32),
            pltpu.SMEM((pair_count + UNROLL,), jnp.int32),
        ],
        name="segment_stack",
    )(tags, chans, offs, where, *rows, *templates)


def local(records, row_dest, row_chan, row_len, templates, tmpl_chan, tmpl_off):
    slot_count, sample_count = records.shape
    size = lax.axis_size("tm")
    half = size // 2
    capacity = slot_count // size
    blocks = sample_count // LANES
    per_block, half_taps, taps = templates.shape
    lags = sample_count - taps - MAXOFF
    me = lax.axis_index("tm")
    side = me // half
    core = lax.axis_index("chan")
    pair_rows = per_block * half_taps

    unit = normalized(templates).reshape(pair_rows * 2, LANES)
    turned = jnp.concatenate([unit[:, :1], jnp.flip(unit[:, 1:], axis=1)], axis=1)
    maps = jnp.concatenate([tmpl_chan.reshape(1, -1), tmpl_off.reshape(1, -1)], axis=1)
    maps = jnp.pad(maps.astype(jnp.float32), ((0, 7), (0, LANES - 2 * pair_rows)))
    block = jnp.concatenate([turned, maps], axis=0)
    shifts = [s for s in range(STOPS)] + [half + s for s in range(STOPS)]
    visiting = {0: block}
    for shift in shifts:
        if shift % size not in visiting:
            visiting[shift % size] = lax.ppermute(
                block, "tm", [(i, (i + shift) % size) for i in range(size)]
            )
    own = [visiting[s % size] for s in range(STOPS)]
    other = [visiting[(half + s) % size] for s in range(STOPS)]

    where = jnp.stack([side, core]).astype(jnp.int32)
    packed = pack_rows(
        records, row_dest, row_chan, row_len, (me % half).reshape(1).astype(jnp.int32), half
    ).reshape(half, 2, capacity, blocks, LANES)
    rows = [packed[0]]
    for step in range(1, half):
        rows.append(
            lax.ppermute(
                packed[step], "tm", [(i, (i // half) * half + ((i % half) ^ step)) for i in range(size)]
            )
        )
    tags = jnp.stack([r[:, :, blocks - 1, LANES - 1] for r in rows], axis=1)
    tags = tags.reshape(2, half * capacity).astype(jnp.int32)
    shape = (half, capacity, blocks, taps, per_block, half_taps, lags)

    def stack_of(group, at):
        maps = jnp.stack([b[2 * pair_rows, : 2 * pair_rows] for b in group]).astype(jnp.int32)
        chans = maps[:, :pair_rows].reshape(-1)
        offs = jnp.pad(maps[:, pair_rows:].reshape(-1), (0, 1))
        return segment_stack(
            rows, group, tags, chans, offs, jnp.stack([at, core]).astype(jnp.int32), shape
        )

    swap = [(0, 1), (1, 0)]
    keep, send = stack_of(other, 1 - side)
    far = keep + lax.ppermute(send, "chan", swap)
    far = lax.ppermute(far, "tm", [(i, (i + half) % size) for i in range(size)])
    keep, send = stack_of(own, side)
    total = keep + lax.ppermute(send, "chan", swap) + far
    return total.reshape(1, STOPS, per_block, lags // 2)


def solution(mesh):
    in_specs = (
        P(("fam", "tm", "chan"), None),
        P(("fam", "tm", "chan")),
        P(("fam", "tm", "chan")),
        P(("fam", "tm", "chan")),
        P(("fam", "tm"), "chan", None),
        P(("fam", "tm"), "chan"),
        P(("fam", "tm"), "chan"),
    )
    out_specs = P(("fam", "tm"), None, None, "chan")
    return jax.shard_map(local, mesh=mesh, in_specs=in_specs, out_specs=out_specs, check_vma=False)
```

```python
import functools

import jax
import jax.numpy as jnp
from jax import lax
from jax.experimental import pallas as pl
from jax.experimental.pallas import tpu as pltpu
from jax.sharding import PartitionSpec as P


TCH = 16
MAXOFF = 256
STOPS = 4
LANES = 128
SUB = 8
UNROLL = 16
PAIR_BITS = 8
SLOT_BITS = 6
PAIR_STEP = 1 << PAIR_BITS
SLOT_STEP = 1 << SLOT_BITS

FLOOR_SHARE = 0.25
TEMPLATE_EPS = 1e-06

SMEM = pl.BlockSpec(memory_space=pltpu.SMEM)
VMEM = pl.BlockSpec(memory_space=pltpu.VMEM)


def split(x):
    high = x.astype(jnp.bfloat16)
    return high, (x - high.astype(jnp.float32)).astype(jnp.bfloat16)


def pack_kernel(half, capacity, dest, chan, length, where, rec, *refs):
    outs = refs[: 2 * half]
    count, source, rows = refs[2 * half :]
    slot_count = dest.shape[0]
    blocks = rec.shape[1] // LANES
    member, home = where[0], where[1]

    def clear_count(i, c):
        count[i] = 0
        return c

    lax.fori_loop(0, count.shape[0], clear_count, 0)

    def clear_source(i, c):
        source[i] = -1
        return c

    lax.fori_loop(0, slot_count, clear_source, 0, unroll=8)

    def place(r, c):
        d = dest[r]
        used = d >= 0
        d = jnp.where(used, d, 2 * half)
        side = jnp.where(d >= half, 1, 0)
        step = jnp.bitwise_xor(d - side * half, member)
        rank = count[d]
        count[d] = rank + 1
        pos = (jnp.where(side == home, half, 0) + step) * capacity + rank
        source[jnp.where(used, pos, slot_count)] = r
        return c

    lax.fori_loop(0, slot_count, place, 0, unroll=8)

    def reform(g, c):
        first = pl.multiple_of(g * SUB, SUB)
        for b in range(blocks):
            rows[pl.ds(first * blocks + b, SUB, stride=blocks), :] = rec[
                pl.ds(first, SUB), b * LANES : (b + 1) * LANES
            ]
        return c

    lax.fori_loop(0, slot_count // SUB, reform, 0)
    flat = lax.broadcasted_iota(jnp.int32, (blocks, LANES), 0) * LANES + lax.broadcasted_iota(
        jnp.int32, (blocks, LANES), 1
    )
    last = blocks * LANES - 1
    for group, out in enumerate(outs):

        def emit(i, c, group=group, out=out):
            r = source[group * capacity + i]
            used = r >= 0
            row = jnp.maximum(r, 0)
            limit = jnp.where(used, length[row], 0)
            tag = jnp.where(used, chan[row], -1).astype(jnp.float32)
            tile = rows[pl.ds(pl.multiple_of(row * blocks, blocks), blocks), :]
            tile = jnp.where(flat < limit, tile, 0.0)
            out[i] = jnp.where(flat == last, tag, tile)
            return c

        lax.fori_loop(0, capacity, emit, 0, unroll=4 if capacity % 4 == 0 else True)


def pack_rows(records, row_dest, row_chan, row_len, where, half):
    slot_count, sample_count = records.shape
    capacity = slot_count // (2 * half)
    blocks = sample_count // LANES
    out = jax.ShapeDtypeStruct((capacity, blocks, LANES), jnp.float32)
    outs = pl.pallas_call(
        functools.partial(pack_kernel, half, capacity),
        out_shape=[out] * (2 * half),
        in_specs=[SMEM] * 4 + [VMEM],
        out_specs=[VMEM] * (2 * half),
        scratch_shapes=[
            pltpu.SMEM((2 * half + 1,), jnp.int32),
            pltpu.SMEM((slot_count + 1,), jnp.int32),
            pltpu.VMEM((slot_count * blocks, LANES), jnp.float32),
        ],
        name="pack_rows",
    )(row_dest, row_chan, row_len, where, records)
    return outs[:half], outs[half:]


def unit_kernel(templ, chan, off, out):
    per_block, half_taps, taps = templ.shape
    pair_rows = per_block * half_taps
    x = templ[...].reshape(pair_rows, taps)
    centred = x - jnp.mean(x, axis=-1, keepdims=True)
    energy = jnp.sum(centred * centred, axis=-1, keepdims=True)
    unit = centred / jnp.sqrt(energy + taps * TEMPLATE_EPS)
    high, rest = split(unit)
    middle, low = split(unit - high.astype(jnp.float32))
    del rest
    row_i = lax.broadcasted_iota(jnp.int32, (LANES, LANES), 0)
    lane_i = lax.broadcasted_iota(jnp.int32, (LANES, LANES), 1)
    turn = jnp.where(row_i == lax.rem(LANES - lane_i, LANES), 1.0, 0.0).astype(jnp.bfloat16)
    for j in range(taps // LANES):
        lanes = slice(j * LANES, (j + 1) * LANES)
        pieces = [
            jnp.dot(part[:, lanes], turn, preferred_element_type=jnp.float32)
            for part in (high, middle, low)
        ]
        out[j * pair_rows : (j + 1) * pair_rows, :] = pieces[0] + (pieces[1] + pieces[2])
    base = (taps // LANES) * pair_rows
    out[base:, :] = jnp.zeros((out.shape[0] - base, LANES), jnp.float32)
    row = jnp.zeros((1, LANES), jnp.float32)
    for which, ref in enumerate((chan, off)):
        for k in range(per_block):
            piece = ref[k : k + 1, :].astype(jnp.float32)
            first = which * pair_rows + k * half_taps
            row += jnp.pad(piece, ((0, 0), (first, LANES - first - half_taps)))
    out[base : base + 1, :] = row


def unit_block(templates, tmpl_chan, tmpl_off):
    per_block, half_taps, taps = templates.shape
    rows = (taps // LANES) * per_block * half_taps + SUB
    return pl.pallas_call(
        unit_kernel,
        out_shape=jax.ShapeDtypeStruct((rows, LANES), jnp.float32),
        in_specs=[VMEM] * 3,
        out_specs=VMEM,
        name="unit_block",
    )(templates, tmpl_chan, tmpl_off)


def segment_kernel(shape, where, *refs):
    parts, capacity, blocks, taps, per_block, half_taps, lags = shape
    rows_in = refs[:parts]
    templ_in = refs[parts : 2 * parts]
    keep, send = refs[2 * parts : 2 * parts + 2]
    (
        x_sc, s_sc, q_sc, inv_sc, h_sc, u_sc, acc, code_v, code_s, listed, sem,
    ) = refs[2 * parts + 2 :]
    segment, member, home, core = where[0], where[1], where[2], where[3]
    size = 2 * parts
    slot_count = parts * capacity
    rows = slot_count * blocks
    pair_rows = per_block * half_taps
    pair_count = STOPS * pair_rows
    block_rows = u_sc.shape[1]
    stack_gain = (taps * TCH) ** 0.5 / TCH

    part_rows = capacity * blocks
    for k in range(parts):
        x_sc[k * part_rows : (k + 1) * part_rows, :] = rows_in[k][...].reshape(part_rows, LANES)
        index = jnp.bitwise_xor(member, k)
        u_sc[home * parts + index] = templ_in[k][:block_rows, :]
        u_sc[(1 - home) * parts + index] = templ_in[k][block_rows:, :]
    x_sc[rows:, :] = jnp.zeros((SUB, LANES), jnp.float32)
    lane_p = lax.broadcasted_iota(jnp.int32, (1, LANES), 1)
    chan_of = jnp.zeros((1, LANES), jnp.float32)
    off_of = jnp.zeros((1, LANES), jnp.float32)
    for s in range(STOPS):
        block = lax.rem(segment - s + size, size)
        maps = u_sc[block, block_rows - SUB : block_rows, :][:1]
        here = lax.div(lane_p, pair_rows) == s
        chan_of = jnp.where(here, pltpu.roll(maps, (s * pair_rows) % LANES, 1), chan_of)
        off_of = jnp.where(here, pltpu.roll(maps, ((s - 1) * pair_rows) % LANES, 1), off_of)
    tags = x_sc[pl.ds(blocks - 1, slot_count, stride=blocks), :][:, LANES - 1 :]
    match = (tags == chan_of).astype(jnp.float32)
    slots = lax.broadcasted_iota(jnp.int32, (slot_count, LANES), 0).astype(jnp.float32)
    slot_of = jnp.sum(match * slots, axis=0, keepdims=True)
    held = jnp.sum(match, axis=0, keepdims=True)
    code = lane_p.astype(jnp.float32) + slot_of * PAIR_STEP + off_of * (PAIR_STEP * SLOT_STEP)
    code = jnp.where(held > 0, code, -1.0).astype(jnp.int32)
    code_v[...] = jnp.broadcast_to(code, (SUB, LANES))
    copy = pltpu.make_async_copy(code_v, code_s, sem)
    copy.start()
    acc[...] = jnp.zeros_like(acc)

    row_i = lax.broadcasted_iota(jnp.int32, (LANES, LANES), 0)
    lane_i = lax.broadcasted_iota(jnp.int32, (LANES, LANES), 1)
    lower = row_i >= lane_i
    tail = lower.astype(jnp.float32).astype(jnp.bfloat16)
    ones = jnp.ones((LANES, LANES), jnp.bfloat16)
    sums = jnp.concatenate([tail, ones], axis=1)
    sums = jnp.concatenate([sums, sums], axis=0)
    chunk_slots = SUB if slot_count % SUB == 0 else 1
    chunk = chunk_slots * blocks

    def prepare(g, c):
        base = pl.multiple_of(g * chunk, chunk)
        x0 = x_sc[pl.ds(base, chunk), :]
        high0, low0 = split(x0)
        s_sc[:chunk, :] = jnp.dot(
            jnp.concatenate([high0, low0], axis=1), sums, preferred_element_type=jnp.float32
        )
        square_high, square_low = split(x0 * x0)
        q_sc[:chunk, :] = jnp.dot(
            jnp.concatenate([square_high, square_low], axis=1),
            sums,
            preferred_element_type=jnp.float32,
        )

        def window(ref):
            return (
                ref[:chunk, :LANES]
                + ref[pl.ds(1, chunk), LANES:]
                + (ref[pl.ds(2, chunk), LANES:] - ref[pl.ds(2, chunk), :LANES])
            )

        win_sum = window(s_sc)
        variance = window(q_sc) - win_sum * win_sum / taps
        inv = stack_gain / jnp.sqrt(jnp.maximum(variance, FLOOR_SHARE * taps))
        inv_sc[pl.ds(base, chunk), :] = inv
        high1, low1 = split(x_sc[pl.ds(base + 1, chunk), :])
        high2, low2 = split(x_sc[pl.ds(base + 2, chunk), :])
        slot0 = g * chunk_slots
        for j, (high, low) in enumerate(((high0, low0), (high1, low1), (high2, low2))):
            lanes = slice(j * LANES, (j + 1) * LANES)
            h_sc[pl.ds(slot0, chunk_slots), :blocks, lanes] = high.reshape(
                chunk_slots, blocks, LANES
            )
            h_sc[pl.ds(slot0, chunk_slots), blocks:, lanes] = low.reshape(
                chunk_slots, blocks, LANES
            )
        return c

    s_sc[chunk:, :] = jnp.zeros((SUB, 2 * LANES), jnp.float32)
    q_sc[chunk:, :] = jnp.zeros((SUB, 2 * LANES), jnp.float32)
    lax.fori_loop(0, slot_count // chunk_slots, prepare, 0)

    copy.wait()

    def gather_pairs(i, filled):
        value = code_s[0, i]
        listed[filled] = value
        return filled + jnp.where(value >= 0, 1, 0)

    filled = lax.fori_loop(0, pair_count, gather_pairs, 0, unroll=16)
    groups = lax.div(filled + UNROLL - 1, UNROLL)
    for i in range(UNROLL):
        listed[filled + i] = pair_count

    lane_b = lax.broadcasted_iota(jnp.int32, (blocks, LANES), 1)
    low_mask = tail > 0
    zero = jnp.zeros((LANES, LANES), jnp.bfloat16)

    def pairs(g, c):
        for j in range(UNROLL):
            value = listed[g * UNROLL + j]
            pair = jnp.bitwise_and(value, PAIR_STEP - 1)
            slot = jnp.bitwise_and(lax.shift_right_logical(value, PAIR_BITS), SLOT_STEP - 1)
            off = lax.shift_right_logical(value, PAIR_BITS + SLOT_BITS)
            stop = lax.div(pair, pair_rows)
            block = lax.rem(segment - stop + size, size)
            inner = pair - stop * pair_rows

            def circulant(row):
                return pltpu.roll(
                    jnp.broadcast_to(u_sc[block, pl.ds(row, 1), :], (LANES, LANES)),
                    0,
                    1,
                    stride=1,
                    stride_axis=0,
                )

            first = split(circulant(inner))
            second = split(circulant(inner + pair_rows))
            bands = [
                jnp.concatenate([jnp.where(low_mask, x, zero) for x in first], axis=1),
                jnp.concatenate(
                    [jnp.where(low_mask, y, x) for x, y in zip(first, second)], axis=1
                ),
                jnp.concatenate([jnp.where(low_mask, zero, y) for y in second], axis=1),
            ]
            weights = jnp.concatenate(bands, axis=0)
            terms = jnp.dot(h_sc[slot], weights, preferred_element_type=jnp.float32)
            corr = (terms[:blocks, :LANES] + terms[:blocks, LANES:]) + (
                terms[blocks:, :LANES] + terms[blocks:, LANES:]
            )
            ratio = corr * inv_sc[pl.ds(pl.multiple_of(slot * blocks, blocks), blocks), :]
            by_lane = jnp.bitwise_and(off, LANES - 1)
            whole = off >= LANES
            here = pltpu.roll(ratio, lax.rem(LANES - by_lane, LANES), 1)
            after = pltpu.roll(here, blocks - 1, 0)
            beyond = pltpu.roll(here, blocks - 2, 0)
            moved = jnp.where(
                lane_b < LANES - by_lane,
                jnp.where(whole, after, here),
                jnp.where(whole, beyond, after),
            )
            acc[lax.div(pair, half_taps)] += moved
        return c

    lax.fori_loop(0, groups, pairs, 0)

    half_lags = lags // 2 // LANES
    for which, ref in ((core, keep), (1 - core, send)):
        for s in range(STOPS):
            stacks = slice(s * per_block, (s + 1) * per_block)
            for b in range(half_lags):
                ref[s, :, b * LANES : (b + 1) * LANES] = jnp.where(
                    which == 0, acc[stacks, b, :], acc[stacks, half_lags + b, :]
                )


def segment_stack(rows, templates, where, shape):
    parts, capacity, blocks, _, per_block, half_taps, lags = shape
    slot_count = parts * capacity
    stack_count = STOPS * per_block
    pair_count = stack_count * half_taps
    chunk = (SUB if slot_count % SUB == 0 else 1) * blocks
    block_rows = templates[0].shape[0] // 2
    out = jax.ShapeDtypeStruct((STOPS, per_block, lags // 2), jnp.float32)
    return pl.pallas_call(
        functools.partial(segment_kernel, shape),
        out_shape=(out, out),
        in_specs=[SMEM] + [VMEM] * (2 * parts),
        out_specs=(VMEM, VMEM),
        scratch_shapes=[
            pltpu.VMEM((slot_count * blocks + SUB, LANES), jnp.float32),
            pltpu.VMEM((chunk + SUB, 2 * LANES), jnp.float32),
            pltpu.VMEM((chunk + SUB, 2 * LANES), jnp.float32),
            pltpu.VMEM((slot_count * blocks, LANES), jnp.float32),
            pltpu.VMEM((slot_count, 2 * blocks, 3 * LANES), jnp.bfloat16),
            pltpu.VMEM((2 * parts, block_rows, LANES), jnp.float32),
            pltpu.VMEM((stack_count + 1, blocks, LANES), jnp.float32),
            pltpu.VMEM((SUB, LANES), jnp.int32),
            pltpu.SMEM((SUB, LANES), jnp.int32),
            pltpu.SMEM((pair_count + UNROLL,), jnp.int32),
            pltpu.SemaphoreType.DMA,
        ],
        name="segment_stack",
    )(where, *rows, *templates)


def local(records, row_dest, row_chan, row_len, templates, tmpl_chan, tmpl_off):
    slot_count, sample_count = records.shape
    size = lax.axis_size("tm")
    half = size // 2
    capacity = slot_count // size
    per_block, half_taps, taps = templates.shape
    lags = sample_count - taps - MAXOFF
    me = lax.axis_index("tm")
    core = lax.axis_index("chan")
    home, member = me // half, me % half
    across = [(i, (i + half) % size) for i in range(size)]
    swap = [(0, 1), (1, 0)]
    shape = (half, capacity, sample_count // LANES, taps, per_block, half_taps, lags)

    def within(x, step):
        return lax.ppermute(
            x, "tm", [(i, (i // half) * half + ((i % half) ^ step)) for i in range(size)]
        )

    far_out, own_out = pack_rows(
        records, row_dest, row_chan, row_len, jnp.stack([member, home]).astype(jnp.int32), half
    )
    far_rows = [far_out[0]] + [within(far_out[k], k) for k in range(1, half)]
    templates, own_out = lax.optimization_barrier((templates, own_out))
    block = unit_block(templates, tmpl_chan, tmpl_off)
    pair = jnp.concatenate([block, lax.ppermute(block, "tm", across)], axis=0)
    pair, own_out = lax.optimization_barrier((pair, own_out))
    blocks = [pair] + [within(pair, k) for k in range(1, half)]
    own_rows = [own_out[0]] + [within(own_out[k], k) for k in range(1, half)]

    def stack_of(rows, segment):
        where = jnp.stack([segment, member, home, core]).astype(jnp.int32)
        return segment_stack(rows, blocks, where, shape)

    keep, send = stack_of(far_rows, (me + half) % size)
    far = keep + lax.ppermute(send, "chan", swap)
    far, *own_rows = lax.optimization_barrier((far, *own_rows))
    far = lax.ppermute(far, "tm", across)
    keep, send = stack_of(own_rows, me)
    total = keep + lax.ppermute(send, "chan", swap) + far
    return total[None]


def solution(mesh):
    in_specs = (
        P(("fam", "tm", "chan"), None),
        P(("fam", "tm", "chan")),
        P(("fam", "tm", "chan")),
        P(("fam", "tm", "chan")),
        P(("fam", "tm"), "chan", None),
        P(("fam", "tm"), "chan"),
        P(("fam", "tm"), "chan"),
    )
    out_specs = P(("fam", "tm"), None, None, "chan")
    return jax.shard_map(local, mesh=mesh, in_specs=in_specs, out_specs=out_specs, check_vma=False)
```

```python
import functools

import jax
import jax.numpy as jnp
from jax import lax
from jax.experimental import pallas as pl
from jax.experimental.pallas import tpu as pltpu
from jax.sharding import PartitionSpec as P


TCH = 16
MAXOFF = 256
STOPS = 4
LANES = 128
HALF = LANES // 2
SUB = 8
UNROLL = 16
PAIR_BITS = 8
SLOT_BITS = 6
PAIR_STEP = 1 << PAIR_BITS
SLOT_STEP = 1 << SLOT_BITS

FLOOR_SHARE = 0.25
TEMPLATE_EPS = 1e-06


SMEM = pl.BlockSpec(memory_space=pltpu.SMEM)
VMEM = pl.BlockSpec(memory_space=pltpu.VMEM)


def split(x):
    high = x.astype(jnp.bfloat16)
    return high, (x - high.astype(jnp.float32)).astype(jnp.bfloat16)


def pack_kernel(half, capacity, dest, chan, length, rec, templ, templ_chan, templ_off, *refs):
    block_out = refs[0]
    outs = refs[1 : 2 * half + 1]
    count, source, raw, rows, stage, in_sems, out_sems = refs[2 * half + 1 :]
    slot_count = dest.shape[0]
    blocks = rec.shape[1] // LANES
    me = lax.axis_index("tm")
    member, home = lax.rem(me, half), lax.div(me, half)
    pieces = in_sems.shape[0]
    piece_rows = slot_count // pieces
    arriving = []
    for p in range(pieces):
        part = pl.ds(p * piece_rows, piece_rows)
        arriving.append(pltpu.make_async_copy(rec.at[part], raw.at[part], in_sems.at[p]))
        arriving[-1].start()
    write_unit(templ, templ_chan, templ_off, block_out)

    def clear_count(i, c):
        count[i] = 0
        return c

    lax.fori_loop(0, count.shape[0], clear_count, 0)

    def clear_source(i, c):
        source[i] = -1
        return c

    lax.fori_loop(0, slot_count, clear_source, 0, unroll=8)

    def place(r, c):
        d = dest[r]
        used = d >= 0
        d = jnp.where(used, d, 2 * half)
        side = jnp.where(d >= half, 1, 0)
        step = jnp.bitwise_xor(d - side * half, member)
        rank = count[d]
        count[d] = rank + 1
        pos = (jnp.where(side == home, half, 0) + step) * capacity + rank
        source[jnp.where(used, pos, slot_count)] = r
        return c

    lax.fori_loop(0, slot_count, place, 0, unroll=8)

    def reform(g, c):
        first = pl.multiple_of(g * SUB, SUB)
        for b in range(blocks):
            rows[pl.ds(first * blocks + b, SUB, stride=blocks), :] = raw[
                pl.ds(first, SUB), b * LANES : (b + 1) * LANES
            ]
        return c

    for p in range(pieces):
        arriving[p].wait()
        lax.fori_loop(p * piece_rows // SUB, (p + 1) * piece_rows // SUB, reform, 0)
    flat = lax.broadcasted_iota(jnp.int32, (blocks, LANES), 0) * LANES + lax.broadcasted_iota(
        jnp.int32, (blocks, LANES), 1
    )
    last = blocks * LANES - 1
    leaving = []
    for group, out in enumerate(outs):

        def emit(i, c, group=group):
            r = source[group * capacity + i]
            used = r >= 0
            row = jnp.maximum(r, 0)
            limit = jnp.where(used, length[row], 0)
            tag = jnp.where(used, chan[row], -1).astype(jnp.float32)
            tile = rows[pl.ds(pl.multiple_of(row * blocks, blocks), blocks), :]
            tile = jnp.where(flat < limit, tile, 0.0)
            stage[group, i * blocks : (i + 1) * blocks, :] = jnp.where(flat == last, tag, tile)
            return c

        for i in range(capacity):
            emit(i, 0)
        if group < half:
            stage[group, capacity * blocks :, :] = block_out[...]
        part = stage.at[group, pl.ds(0, out.shape[0])]
        leaving.append(pltpu.make_async_copy(part, out, out_sems.at[group]))
        leaving[-1].start()
    for copy in leaving:
        copy.wait()


def write_unit(templ, chan, off, out):
    per_block, half_taps, taps = templ.shape
    pair_rows = per_block * half_taps
    x = templ[...].reshape(pair_rows, taps)
    centred = x - jnp.mean(x, axis=-1, keepdims=True)
    energy = jnp.sum(centred * centred, axis=-1, keepdims=True)
    unit = centred / jnp.sqrt(energy + taps * TEMPLATE_EPS)
    high, rest = split(unit)
    middle, low = split(unit - high.astype(jnp.float32))
    del rest
    row_i = lax.broadcasted_iota(jnp.int32, (LANES, LANES), 0)
    lane_i = lax.broadcasted_iota(jnp.int32, (LANES, LANES), 1)
    turn = jnp.where(row_i == lax.rem(LANES - lane_i, LANES), 1.0, 0.0).astype(jnp.bfloat16)
    for j in range(taps // LANES):
        lanes = slice(j * LANES, (j + 1) * LANES)
        pieces = [
            jnp.dot(part[:, lanes], turn, preferred_element_type=jnp.float32)
            for part in (high, middle, low)
        ]
        out[j * pair_rows : (j + 1) * pair_rows, :] = pieces[0] + (pieces[1] + pieces[2])
    base = (taps // LANES) * pair_rows
    out[base:, :] = jnp.zeros((out.shape[0] - base, LANES), jnp.float32)
    row = jnp.zeros((1, LANES), jnp.float32)
    for which, ref in enumerate((chan, off)):
        for k in range(per_block):
            piece = ref[k : k + 1, :].astype(jnp.float32)
            first = which * pair_rows + k * half_taps
            row += jnp.pad(piece, ((0, 0), (first, LANES - first - half_taps)))
    out[base : base + 1, :] = row


def pack(records, row_dest, row_chan, row_len, templates, tmpl_chan, tmpl_off, half):
    slot_count, sample_count = records.shape
    capacity = slot_count // (2 * half)
    blocks = sample_count // LANES
    per_block, half_taps, taps = templates.shape
    block_rows = (taps // LANES) * per_block * half_taps + SUB
    pieces = 4 if slot_count % (4 * SUB) == 0 else 1
    far = jax.ShapeDtypeStruct((capacity * blocks + block_rows, LANES), jnp.float32)
    own = jax.ShapeDtypeStruct((capacity * blocks, LANES), jnp.float32)
    whole = pl.BlockSpec(memory_space=pl.ANY)
    block, *outs = pl.pallas_call(
        functools.partial(pack_kernel, half, capacity),
        out_shape=[jax.ShapeDtypeStruct((block_rows, LANES), jnp.float32)]
        + [far] * half
        + [own] * half,
        in_specs=[SMEM] * 3 + [whole] + [VMEM] * 3,
        out_specs=[VMEM] + [whole] * (2 * half),
        scratch_shapes=[
            pltpu.SMEM((2 * half + 1,), jnp.int32),
            pltpu.SMEM((slot_count + 1,), jnp.int32),
            pltpu.VMEM((slot_count, sample_count), jnp.float32),
            pltpu.VMEM((slot_count * blocks, LANES), jnp.float32),
            pltpu.VMEM((2 * half, capacity * blocks + block_rows, LANES), jnp.float32),
            pltpu.SemaphoreType.DMA((pieces,)),
            pltpu.SemaphoreType.DMA((2 * half,)),
        ],
        name="pack",
    )(row_dest, row_chan, row_len, records, templates, tmpl_chan, tmpl_off)
    return block, outs[:half], outs[half:]


def segment_kernel(shape, ahead, *refs):
    parts, capacity, blocks, taps, per_block, half_taps, lags = shape
    count = len(refs) - 14
    rows_in = refs[:parts]
    near_in = refs[:parts] if count == 2 * parts else refs[parts : 2 * parts]
    other_in = refs[count - parts : count]
    keep, send = refs[count : count + 2]
    (
        x_sc, y_sc, s_sc, q_sc, inv_sc, h_sc, u_sc, acc, code_v, code_s, listed, sems,
    ) = refs[count + 2 :]
    size = 2 * parts
    me = lax.axis_index("tm")
    core = lax.axis_index("chan")
    segment = lax.rem(me + ahead, size)
    member, home = lax.rem(me, parts), lax.div(me, parts)
    slot_count = parts * capacity
    rows = slot_count * blocks
    pair_rows = per_block * half_taps
    pair_count = STOPS * pair_rows
    block_rows = u_sc.shape[1]
    stack_gain = (taps * TCH) ** 0.5 / TCH

    part_rows = capacity * blocks
    copies = []
    for k in range(parts):
        index = jnp.bitwise_xor(member, k)
        moves = (
            (rows_in[k].at[pl.ds(0, part_rows)], x_sc.at[pl.ds(k * part_rows, part_rows)]),
            (near_in[k].at[pl.ds(part_rows, block_rows)], u_sc.at[home * parts + index]),
            (other_in[k], u_sc.at[(1 - home) * parts + index]),
        )
        for source, target in moves:
            copies.append(pltpu.make_async_copy(source, target, sems.at[1 + len(copies)]))
            copies[-1].start()
    x_sc[rows:, :] = jnp.zeros((SUB, LANES), jnp.float32)
    acc[...] = jnp.zeros_like(acc)
    for copy in copies:
        copy.wait()

    lane_p = lax.broadcasted_iota(jnp.int32, (1, LANES), 1)
    chan_of = jnp.zeros((1, LANES), jnp.float32)
    off_of = jnp.zeros((1, LANES), jnp.float32)
    for s in range(STOPS):
        maps = u_sc[lax.rem(segment - s + size, size), block_rows - SUB : block_rows, :][:1]
        here = lax.div(lane_p, pair_rows) == s
        chan_of = jnp.where(here, pltpu.roll(maps, (s * pair_rows) % LANES, 1), chan_of)
        off_of = jnp.where(here, pltpu.roll(maps, ((s - 1) * pair_rows) % LANES, 1), off_of)
    tags = x_sc[pl.ds(blocks - 1, slot_count, stride=blocks), :][:, LANES - 1 :]
    match = (tags == chan_of).astype(jnp.float32)
    slots = lax.broadcasted_iota(jnp.int32, (slot_count, LANES), 0).astype(jnp.float32)
    slot_of = jnp.sum(match * slots, axis=0, keepdims=True)
    held = jnp.sum(match, axis=0, keepdims=True)
    code = lane_p.astype(jnp.float32) + slot_of * PAIR_STEP + off_of * (PAIR_STEP * SLOT_STEP)
    code = jnp.where(held > 0, code, -1.0).astype(jnp.int32)
    code_v[...] = jnp.broadcast_to(code, (SUB, LANES))
    copy = pltpu.make_async_copy(code_v, code_s, sems.at[0])
    copy.start()

    row_i = lax.broadcasted_iota(jnp.int32, (LANES, LANES), 0)
    lane_i = lax.broadcasted_iota(jnp.int32, (LANES, LANES), 1)
    lower = row_i >= lane_i
    tail = lower.astype(jnp.float32).astype(jnp.bfloat16)
    ones = jnp.ones((LANES, LANES), jnp.bfloat16)
    sums = jnp.concatenate([tail, ones], axis=1)
    sums = jnp.concatenate([sums, sums], axis=0)
    chunk_slots = SUB if slot_count % SUB == 0 else 1
    chunk = chunk_slots * blocks

    def prepare(g, c):
        base = pl.multiple_of(g * chunk, chunk)
        x0 = x_sc[pl.ds(base, chunk), :]
        high0, low0 = split(x0)
        s_sc[:chunk, :] = jnp.dot(
            jnp.concatenate([high0, low0], axis=1), sums, preferred_element_type=jnp.float32
        )
        square_high, square_low = split(x0 * x0)
        q_sc[:chunk, :] = jnp.dot(
            jnp.concatenate([square_high, square_low], axis=1),
            sums,
            preferred_element_type=jnp.float32,
        )

        def window(ref):
            return (
                ref[:chunk, :LANES]
                + ref[pl.ds(1, chunk), LANES:]
                + (ref[pl.ds(2, chunk), LANES:] - ref[pl.ds(2, chunk), :LANES])
            )

        win_sum = window(s_sc)
        variance = window(q_sc) - win_sum * win_sum / taps
        inv = stack_gain / jnp.sqrt(jnp.maximum(variance, FLOOR_SHARE * taps))
        inv_sc[pl.ds(base, chunk), :] = inv
        before = y_sc[pl.ds(base + SUB - 1, chunk), :]
        after = y_sc[pl.ds(base + SUB + 1, chunk), :]
        windows = (
            (jnp.where(left, x0, after), x_sc[pl.ds(base + 2, chunk), :]),
            (jnp.where(left, before, x0), after),
        )
        slot0 = g * chunk_slots
        for i, window_pair in enumerate(windows):
            for j, part in enumerate(window_pair):
                lanes = slice(j * LANES, (j + 1) * LANES)
                for k, piece in enumerate(split(part)):
                    first = (2 * i + k) * blocks
                    h_sc[pl.ds(slot0, chunk_slots), first : first + blocks, lanes] = piece.reshape(
                        chunk_slots, blocks, LANES
                    )
        return c

    s_sc[chunk:, :] = jnp.zeros((SUB, 2 * LANES), jnp.float32)
    q_sc[chunk:, :] = jnp.zeros((SUB, 2 * LANES), jnp.float32)
    left = lax.broadcasted_iota(jnp.int32, (chunk, LANES), 1) < HALF

    def turn(g, c):
        base = pl.multiple_of(g * chunk, chunk)
        y_sc[pl.ds(base + SUB, chunk), :] = pltpu.roll(x_sc[pl.ds(base, chunk), :], HALF, 1)
        return c

    y_sc[:SUB, :] = jnp.zeros((SUB, LANES), jnp.float32)
    y_sc[rows + SUB :, :] = jnp.zeros((SUB, LANES), jnp.float32)
    lax.fori_loop(0, slot_count // chunk_slots, turn, 0)
    lax.fori_loop(0, slot_count // chunk_slots, prepare, 0)

    copy.wait()

    def gather_pairs(i, filled):
        value = code_s[0, i]
        listed[filled] = value
        return filled + jnp.where(value >= 0, 1, 0)

    filled = lax.fori_loop(0, pair_count, gather_pairs, 0, unroll=16)
    groups = lax.div(filled + UNROLL - 1, UNROLL)
    for i in range(UNROLL):
        listed[filled + i] = pair_count

    lane_b = lax.broadcasted_iota(jnp.int32, (blocks, LANES), 1)
    row_h = lax.broadcasted_iota(jnp.int32, (HALF, LANES), 0)
    lane_h = lax.broadcasted_iota(jnp.int32, (HALF, LANES), 1)
    mask = (row_h >= lane_h).astype(jnp.float32).astype(jnp.bfloat16) > 0
    zero = jnp.zeros((HALF, LANES), jnp.bfloat16)
    left_b = lane_b < HALF

    def pairs(g, c):
        for j in range(UNROLL):
            value = listed[g * UNROLL + j]
            pair = jnp.bitwise_and(value, PAIR_STEP - 1)
            slot = jnp.bitwise_and(lax.shift_right_logical(value, PAIR_BITS), SLOT_STEP - 1)
            off = lax.shift_right_logical(value, PAIR_BITS + SLOT_BITS)
            stop = lax.div(pair, pair_rows)
            block = lax.rem(segment - stop + size, size)
            inner = pair - stop * pair_rows

            def circulant(row):
                return pltpu.roll(
                    jnp.broadcast_to(u_sc[block, pl.ds(row, 1), :], (HALF, LANES)),
                    0,
                    1,
                    stride=1,
                    stride_axis=0,
                )

            first = split(circulant(inner))
            second = split(circulant(inner + pair_rows))
            bands = [
                jnp.concatenate([jnp.where(mask, x, zero) for x in first], axis=1),
                jnp.concatenate([jnp.where(mask, y, x) for x, y in zip(first, second)], axis=1),
                jnp.concatenate([jnp.where(mask, zero, y) for y in second], axis=1),
            ]
            terms = jnp.dot(
                h_sc[slot, :, : 3 * HALF],
                jnp.concatenate(bands, axis=0),
                preferred_element_type=jnp.float32,
            )
            front, back = (
                (part[:blocks, :LANES] + part[:blocks, LANES:])
                + (part[blocks:, :LANES] + part[blocks:, LANES:])
                for part in (terms[: 2 * blocks], terms[2 * blocks :])
            )
            back = jnp.where(left_b, pltpu.roll(back, blocks - 1, 0), back)
            corr = front + pltpu.roll(back, HALF, 1)
            ratio = corr * inv_sc[pl.ds(pl.multiple_of(slot * blocks, blocks), blocks), :]
            by_lane = jnp.bitwise_and(off, LANES - 1)
            whole = off >= LANES
            here = pltpu.roll(ratio, lax.rem(LANES - by_lane, LANES), 1)
            after = pltpu.roll(here, blocks - 1, 0)
            beyond = pltpu.roll(here, blocks - 2, 0)
            moved = jnp.where(
                lane_b < LANES - by_lane,
                jnp.where(whole, after, here),
                jnp.where(whole, beyond, after),
            )
            acc[lax.div(pair, half_taps)] += moved
        return c

    lax.fori_loop(0, groups, pairs, 0)

    half_lags = lags // 2 // LANES
    for which, ref in ((core, keep), (1 - core, send)):
        for s in range(STOPS):
            stacks = slice(s * per_block, (s + 1) * per_block)
            for b in range(half_lags):
                ref[s, :, b * LANES : (b + 1) * LANES] = jnp.where(
                    which == 0, acc[stacks, b, :], acc[stacks, half_lags + b, :]
                )


def segment_stack(rows, near, other, ahead, shape):
    parts, capacity, blocks, _, per_block, half_taps, lags = shape
    slot_count = parts * capacity
    stack_count = STOPS * per_block
    pair_count = stack_count * half_taps
    chunk = (SUB if slot_count % SUB == 0 else 1) * blocks
    block_rows = other[0].shape[0]
    out = jax.ShapeDtypeStruct((STOPS, per_block, lags // 2), jnp.float32)
    operands = list(rows) + ([] if near is rows else list(near)) + list(other)
    return pl.pallas_call(
        functools.partial(segment_kernel, shape, ahead),
        out_shape=(out, out),
        in_specs=[pl.BlockSpec(memory_space=pltpu.HBM)] * len(operands),
        out_specs=(VMEM, VMEM),
        scratch_shapes=[
            pltpu.VMEM((slot_count * blocks + SUB, LANES), jnp.float32),
            pltpu.VMEM((slot_count * blocks + 2 * SUB, LANES), jnp.float32),
            pltpu.VMEM((chunk + SUB, 2 * LANES), jnp.float32),
            pltpu.VMEM((chunk + SUB, 2 * LANES), jnp.float32),
            pltpu.VMEM((slot_count * blocks, LANES), jnp.float32),
            pltpu.VMEM((slot_count, 4 * blocks, 2 * LANES), jnp.bfloat16),
            pltpu.VMEM((2 * parts, block_rows, LANES), jnp.float32),
            pltpu.VMEM((stack_count + 1, blocks, LANES), jnp.float32),
            pltpu.VMEM((SUB, LANES), jnp.int32),
            pltpu.SMEM((SUB, LANES), jnp.int32),
            pltpu.SMEM((pair_count + UNROLL,), jnp.int32),
            pltpu.SemaphoreType.DMA((3 * parts + 1,)),
        ],
        name="segment_stack",
    )(*operands)


def local(records, row_dest, row_chan, row_len, templates, tmpl_chan, tmpl_off):
    slot_count, sample_count = records.shape
    size = lax.axis_size("tm")
    half = size // 2
    capacity = slot_count // size
    per_block, half_taps, taps = templates.shape
    lags = sample_count - taps - MAXOFF
    across = [(i, (i + half) % size) for i in range(size)]
    swap = [(0, 1), (1, 0)]
    shape = (half, capacity, sample_count // LANES, taps, per_block, half_taps, lags)

    def within(x, step):
        return lax.ppermute(
            x, "tm", [(i, (i // half) * half + ((i % half) ^ step)) for i in range(size)]
        )

    block, far_out, own_out = pack(
        records, row_dest, row_chan, row_len, templates, tmpl_chan, tmpl_off, half
    )

    far_rows = [far_out[0]] + [within(far_out[k], k) for k in range(1, half)]
    other = [
        lax.ppermute(block, "tm", [(i, (i ^ k) ^ half) for i in range(size)])
        for k in range(half)
    ]
    own_rows = [own_out[0]] + [within(own_out[k], k) for k in range(1, half)]
    keep, send = segment_stack(far_rows, far_rows, other, half, shape)
    far = keep + lax.ppermute(send, "chan", swap)
    far, *own_rows = lax.optimization_barrier((far, *own_rows))
    far = lax.ppermute(far, "tm", across)
    keep, send = segment_stack(own_rows, far_rows, other, 0, shape)
    total = keep + lax.ppermute(send, "chan", swap) + far
    return total[None]


def solution(mesh):
    in_specs = (
        P(("fam", "tm", "chan"), None),
        P(("fam", "tm", "chan")),
        P(("fam", "tm", "chan")),
        P(("fam", "tm", "chan")),
        P(("fam", "tm"), "chan", None),
        P(("fam", "tm"), "chan"),
        P(("fam", "tm"), "chan"),
    )
    out_specs = P(("fam", "tm"), None, None, "chan")
    return jax.shard_map(local, mesh=mesh, in_specs=in_specs, out_specs=out_specs, check_vma=False)
```

```python
import functools

import jax
import jax.numpy as jnp
from jax import lax
from jax.experimental import pallas as pl
from jax.experimental.pallas import tpu as pltpu
from jax.sharding import PartitionSpec as P


TCH = 16
MAXOFF = 256
STOPS = 4
LANES = 128
HALF = LANES // 2
SUB = 8
UNROLL = 16
PAIR_BITS = 8
SLOT_BITS = 6
PAIR_STEP = 1 << PAIR_BITS
SLOT_STEP = 1 << SLOT_BITS

FLOOR_SHARE = 0.25
TEMPLATE_EPS = 1e-06


SMEM = pl.BlockSpec(memory_space=pltpu.SMEM)
VMEM = pl.BlockSpec(memory_space=pltpu.VMEM)
KERNEL_BYTES = 24 << 20


def in_main(arrays):
    return [pltpu.with_memory_space_constraint(x, pltpu.HBM) for x in arrays]


def on_chip(arrays):
    return [pltpu.with_memory_space_constraint(x, pltpu.VMEM) for x in arrays]


def split(x):
    high = x.astype(jnp.bfloat16)
    return high, (x - high.astype(jnp.float32)).astype(jnp.bfloat16)


def pack_kernel(half, capacity, dest, chan, length, rec, templ, templ_chan, templ_off, *refs):
    block_out = refs[0]
    outs = refs[1 : 2 * half + 1]
    count, source, raw, rows, in_sems = refs[2 * half + 1 :]
    slot_count = dest.shape[0]
    blocks = rec.shape[1] // LANES
    me = lax.axis_index("tm")
    member, home = lax.rem(me, half), lax.div(me, half)
    pieces = in_sems.shape[0]
    piece_rows = slot_count // pieces
    arriving = []
    for p in range(pieces):
        part = pl.ds(p * piece_rows, piece_rows)
        arriving.append(pltpu.make_async_copy(rec.at[part], raw.at[part], in_sems.at[p]))
        arriving[-1].start()
    write_unit(templ, templ_chan, templ_off, block_out)

    def clear_count(i, c):
        count[i] = 0
        return c

    lax.fori_loop(0, count.shape[0], clear_count, 0)

    def clear_source(i, c):
        source[i] = -1
        return c

    lax.fori_loop(0, slot_count, clear_source, 0, unroll=8)

    def place(r, c):
        d = dest[r]
        used = d >= 0
        d = jnp.where(used, d, 2 * half)
        side = jnp.where(d >= half, 1, 0)
        step = jnp.bitwise_xor(d - side * half, member)
        rank = count[d]
        count[d] = rank + 1
        pos = (jnp.where(side == home, half, 0) + step) * capacity + rank
        source[jnp.where(used, pos, slot_count)] = r
        return c

    lax.fori_loop(0, slot_count, place, 0, unroll=8)

    def reform(g, c):
        first = pl.multiple_of(g * SUB, SUB)
        for b in range(blocks):
            rows[pl.ds(first * blocks + b, SUB, stride=blocks), :] = raw[
                pl.ds(first, SUB), b * LANES : (b + 1) * LANES
            ]
        return c

    for p in range(pieces):
        arriving[p].wait()
        lax.fori_loop(p * piece_rows // SUB, (p + 1) * piece_rows // SUB, reform, 0)
    flat = lax.broadcasted_iota(jnp.int32, (blocks, LANES), 0) * LANES + lax.broadcasted_iota(
        jnp.int32, (blocks, LANES), 1
    )
    last = blocks * LANES - 1
    for group, out in enumerate(outs):

        def emit(i, c, group=group, out=out):
            r = source[group * capacity + i]
            used = r >= 0
            row = jnp.maximum(r, 0)
            limit = jnp.where(used, length[row], 0)
            tag = jnp.where(used, chan[row], -1).astype(jnp.float32)
            tile = rows[pl.ds(pl.multiple_of(row * blocks, blocks), blocks), :]
            tile = jnp.where(flat < limit, tile, 0.0)
            out[i * blocks : (i + 1) * blocks, :] = jnp.where(flat == last, tag, tile)
            return c

        for i in range(capacity):
            emit(i, 0)
        if group < half:
            out[capacity * blocks :, :] = block_out[...]


def write_unit(templ, chan, off, out):
    per_block, half_taps, taps = templ.shape
    pair_rows = per_block * half_taps
    x = templ[...].reshape(pair_rows, taps)
    centred = x - jnp.mean(x, axis=-1, keepdims=True)
    energy = jnp.sum(centred * centred, axis=-1, keepdims=True)
    unit = centred / jnp.sqrt(energy + taps * TEMPLATE_EPS)
    high, rest = split(unit)
    middle, low = split(unit - high.astype(jnp.float32))
    del rest
    row_i = lax.broadcasted_iota(jnp.int32, (LANES, LANES), 0)
    lane_i = lax.broadcasted_iota(jnp.int32, (LANES, LANES), 1)
    turn = jnp.where(row_i == lax.rem(LANES - lane_i, LANES), 1.0, 0.0).astype(jnp.bfloat16)
    for j in range(taps // LANES):
        lanes = slice(j * LANES, (j + 1) * LANES)
        pieces = [
            jnp.dot(part[:, lanes], turn, preferred_element_type=jnp.float32)
            for part in (high, middle, low)
        ]
        out[j * pair_rows : (j + 1) * pair_rows, :] = pieces[0] + (pieces[1] + pieces[2])
    base = (taps // LANES) * pair_rows
    out[base:, :] = jnp.zeros((out.shape[0] - base, LANES), jnp.float32)
    row = jnp.zeros((1, LANES), jnp.float32)
    for which, ref in enumerate((chan, off)):
        for k in range(per_block):
            piece = ref[k : k + 1, :].astype(jnp.float32)
            first = which * pair_rows + k * half_taps
            row += jnp.pad(piece, ((0, 0), (first, LANES - first - half_taps)))
    out[base : base + 1, :] = row


def pack(records, row_dest, row_chan, row_len, templates, tmpl_chan, tmpl_off, half):
    slot_count, sample_count = records.shape
    capacity = slot_count // (2 * half)
    blocks = sample_count // LANES
    per_block, half_taps, taps = templates.shape
    block_rows = (taps // LANES) * per_block * half_taps + SUB
    pieces = 4 if slot_count % (4 * SUB) == 0 else 1
    far = pltpu.VMEM((capacity * blocks + block_rows, LANES), jnp.float32)
    own = pltpu.VMEM((capacity * blocks, LANES), jnp.float32)
    whole = pl.BlockSpec(memory_space=pl.ANY)
    block, *outs = pl.pallas_call(
        functools.partial(pack_kernel, half, capacity),
        out_shape=[pltpu.VMEM((block_rows, LANES), jnp.float32)]
        + [far] * half
        + [own] * half,
        in_specs=[SMEM] * 3 + [whole] + [VMEM] * 3,
        out_specs=[VMEM] * (2 * half + 1),
        scratch_shapes=[
            pltpu.SMEM((2 * half + 1,), jnp.int32),
            pltpu.SMEM((slot_count + 1,), jnp.int32),
            pltpu.VMEM((slot_count, sample_count), jnp.float32),
            pltpu.VMEM((slot_count * blocks, LANES), jnp.float32),
            pltpu.SemaphoreType.DMA((pieces,)),
        ],
        compiler_params=pltpu.CompilerParams(vmem_limit_bytes=KERNEL_BYTES),
        name="pack",
    )(*in_main((row_dest, row_chan, row_len, records, templates, tmpl_chan, tmpl_off)))
    return block, outs[:half], outs[half:]


def segment_kernel(shape, ahead, *refs):
    parts, capacity, blocks, taps, per_block, half_taps, lags = shape
    count = len(refs) - 14
    rows_in = refs[:parts]
    near_in = refs[:parts] if count == 2 * parts else refs[parts : 2 * parts]
    other_in = refs[count - parts : count]
    keep, send = refs[count : count + 2]
    (
        x_sc, y_sc, s_sc, q_sc, inv_sc, h_sc, u_sc, acc, code_v, code_s, listed, sems,
    ) = refs[count + 2 :]
    size = 2 * parts
    me = lax.axis_index("tm")
    core = lax.axis_index("chan")
    segment = lax.rem(me + ahead, size)
    member, home = lax.rem(me, parts), lax.div(me, parts)
    slot_count = parts * capacity
    rows = slot_count * blocks
    pair_rows = per_block * half_taps
    pair_count = STOPS * pair_rows
    block_rows = u_sc.shape[1]
    stack_gain = (taps * TCH) ** 0.5 / TCH

    part_rows = capacity * blocks
    for k in range(parts):
        index = jnp.bitwise_xor(member, k)
        x_sc[k * part_rows : (k + 1) * part_rows, :] = rows_in[k][:part_rows, :]
        u_sc[home * parts + index] = near_in[k][part_rows:, :]
        u_sc[(1 - home) * parts + index] = other_in[k][...]
    x_sc[rows:, :] = jnp.zeros((SUB, LANES), jnp.float32)
    acc[...] = jnp.zeros_like(acc)

    lane_p = lax.broadcasted_iota(jnp.int32, (1, LANES), 1)
    chan_of = jnp.zeros((1, LANES), jnp.float32)
    off_of = jnp.zeros((1, LANES), jnp.float32)
    for s in range(STOPS):
        maps = u_sc[lax.rem(segment - s + size, size), block_rows - SUB : block_rows, :][:1]
        here = lax.div(lane_p, pair_rows) == s
        chan_of = jnp.where(here, pltpu.roll(maps, (s * pair_rows) % LANES, 1), chan_of)
        off_of = jnp.where(here, pltpu.roll(maps, ((s - 1) * pair_rows) % LANES, 1), off_of)
    tags = x_sc[pl.ds(blocks - 1, slot_count, stride=blocks), :][:, LANES - 1 :]
    match = (tags == chan_of).astype(jnp.float32)
    slots = lax.broadcasted_iota(jnp.int32, (slot_count, LANES), 0).astype(jnp.float32)
    slot_of = jnp.sum(match * slots, axis=0, keepdims=True)
    held = jnp.sum(match, axis=0, keepdims=True)
    code = lane_p.astype(jnp.float32) + slot_of * PAIR_STEP + off_of * (PAIR_STEP * SLOT_STEP)
    code = jnp.where(held > 0, code, -1.0).astype(jnp.int32)
    code_v[...] = jnp.broadcast_to(code, (SUB, LANES))
    copy = pltpu.make_async_copy(code_v, code_s, sems.at[0])
    copy.start()

    row_i = lax.broadcasted_iota(jnp.int32, (LANES, LANES), 0)
    lane_i = lax.broadcasted_iota(jnp.int32, (LANES, LANES), 1)
    lower = row_i >= lane_i
    tail = lower.astype(jnp.float32).astype(jnp.bfloat16)
    ones = jnp.ones((LANES, LANES), jnp.bfloat16)
    sums = jnp.concatenate([tail, ones], axis=1)
    sums = jnp.concatenate([sums, sums], axis=0)
    chunk_slots = SUB if slot_count % SUB == 0 else 1
    chunk = chunk_slots * blocks

    def prepare(g, c):
        base = pl.multiple_of(g * chunk, chunk)
        x0 = x_sc[pl.ds(base, chunk), :]
        high0, low0 = split(x0)
        s_sc[:chunk, :] = jnp.dot(
            jnp.concatenate([high0, low0], axis=1), sums, preferred_element_type=jnp.float32
        )
        square_high, square_low = split(x0 * x0)
        q_sc[:chunk, :] = jnp.dot(
            jnp.concatenate([square_high, square_low], axis=1),
            sums,
            preferred_element_type=jnp.float32,
        )

        def window(ref):
            return (
                ref[:chunk, :LANES]
                + ref[pl.ds(1, chunk), LANES:]
                + (ref[pl.ds(2, chunk), LANES:] - ref[pl.ds(2, chunk), :LANES])
            )

        win_sum = window(s_sc)
        variance = window(q_sc) - win_sum * win_sum / taps
        inv = stack_gain / jnp.sqrt(jnp.maximum(variance, FLOOR_SHARE * taps))
        inv_sc[pl.ds(base, chunk), :] = inv
        before = y_sc[pl.ds(base + SUB - 1, chunk), :]
        after = y_sc[pl.ds(base + SUB + 1, chunk), :]
        windows = (
            (jnp.where(left, x0, after), x_sc[pl.ds(base + 2, chunk), :]),
            (jnp.where(left, before, x0), after),
        )
        slot0 = g * chunk_slots
        for i, window_pair in enumerate(windows):
            for j, part in enumerate(window_pair):
                lanes = slice(j * LANES, (j + 1) * LANES)
                for k, piece in enumerate(split(part)):
                    first = (2 * i + k) * blocks
                    h_sc[pl.ds(slot0, chunk_slots), first : first + blocks, lanes] = piece.reshape(
                        chunk_slots, blocks, LANES
                    )
        return c

    s_sc[chunk:, :] = jnp.zeros((SUB, 2 * LANES), jnp.float32)
    q_sc[chunk:, :] = jnp.zeros((SUB, 2 * LANES), jnp.float32)
    left = lax.broadcasted_iota(jnp.int32, (chunk, LANES), 1) < HALF

    def turn(g, c):
        base = pl.multiple_of(g * chunk, chunk)
        y_sc[pl.ds(base + SUB, chunk), :] = pltpu.roll(x_sc[pl.ds(base, chunk), :], HALF, 1)
        return c

    y_sc[:SUB, :] = jnp.zeros((SUB, LANES), jnp.float32)
    y_sc[rows + SUB :, :] = jnp.zeros((SUB, LANES), jnp.float32)
    lax.fori_loop(0, slot_count // chunk_slots, turn, 0)
    lax.fori_loop(0, slot_count // chunk_slots, prepare, 0)

    copy.wait()

    def gather_pairs(i, filled):
        value = code_s[0, i]
        listed[filled] = value
        return filled + jnp.where(value >= 0, 1, 0)

    filled = lax.fori_loop(0, pair_count, gather_pairs, 0, unroll=16)
    groups = lax.div(filled + UNROLL - 1, UNROLL)
    for i in range(UNROLL):
        listed[filled + i] = pair_count

    lane_b = lax.broadcasted_iota(jnp.int32, (blocks, LANES), 1)
    row_h = lax.broadcasted_iota(jnp.int32, (HALF, LANES), 0)
    lane_h = lax.broadcasted_iota(jnp.int32, (HALF, LANES), 1)
    mask = (row_h >= lane_h).astype(jnp.float32).astype(jnp.bfloat16) > 0
    zero = jnp.zeros((HALF, LANES), jnp.bfloat16)
    left_b = lane_b < HALF

    def pairs(g, c):
        for j in range(UNROLL):
            value = listed[g * UNROLL + j]
            pair = jnp.bitwise_and(value, PAIR_STEP - 1)
            slot = jnp.bitwise_and(lax.shift_right_logical(value, PAIR_BITS), SLOT_STEP - 1)
            off = lax.shift_right_logical(value, PAIR_BITS + SLOT_BITS)
            stop = lax.div(pair, pair_rows)
            block = lax.rem(segment - stop + size, size)
            inner = pair - stop * pair_rows

            def circulant(row):
                return pltpu.roll(
                    jnp.broadcast_to(u_sc[block, pl.ds(row, 1), :], (HALF, LANES)),
                    0,
                    1,
                    stride=1,
                    stride_axis=0,
                )

            first = split(circulant(inner))
            second = split(circulant(inner + pair_rows))
            bands = [
                jnp.concatenate([jnp.where(mask, x, zero) for x in first], axis=1),
                jnp.concatenate([jnp.where(mask, y, x) for x, y in zip(first, second)], axis=1),
                jnp.concatenate([jnp.where(mask, zero, y) for y in second], axis=1),
            ]
            terms = jnp.dot(
                h_sc[slot, :, : 3 * HALF],
                jnp.concatenate(bands, axis=0),
                preferred_element_type=jnp.float32,
            )
            front, back = (
                (part[:blocks, :LANES] + part[:blocks, LANES:])
                + (part[blocks:, :LANES] + part[blocks:, LANES:])
                for part in (terms[: 2 * blocks], terms[2 * blocks :])
            )
            back = jnp.where(left_b, pltpu.roll(back, blocks - 1, 0), back)
            corr = front + pltpu.roll(back, HALF, 1)
            ratio = corr * inv_sc[pl.ds(pl.multiple_of(slot * blocks, blocks), blocks), :]
            by_lane = jnp.bitwise_and(off, LANES - 1)
            whole = off >= LANES
            here = pltpu.roll(ratio, lax.rem(LANES - by_lane, LANES), 1)
            after = pltpu.roll(here, blocks - 1, 0)
            beyond = pltpu.roll(here, blocks - 2, 0)
            moved = jnp.where(
                lane_b < LANES - by_lane,
                jnp.where(whole, after, here),
                jnp.where(whole, beyond, after),
            )
            acc[lax.div(pair, half_taps)] += moved
        return c

    lax.fori_loop(0, groups, pairs, 0)

    half_lags = lags // 2 // LANES
    for which, ref in ((core, keep), (1 - core, send)):
        for s in range(STOPS):
            stacks = slice(s * per_block, (s + 1) * per_block)
            for b in range(half_lags):
                ref[s, :, b * LANES : (b + 1) * LANES] = jnp.where(
                    which == 0, acc[stacks, b, :], acc[stacks, half_lags + b, :]
                )


def segment_stack(rows, near, other, ahead, shape):
    parts, capacity, blocks, _, per_block, half_taps, lags = shape
    slot_count = parts * capacity
    stack_count = STOPS * per_block
    pair_count = stack_count * half_taps
    chunk = (SUB if slot_count % SUB == 0 else 1) * blocks
    block_rows = other[0].shape[0]
    out = pltpu.VMEM((STOPS, per_block, lags // 2), jnp.float32)
    operands = list(rows) + ([] if near is rows else list(near)) + list(other)
    return pl.pallas_call(
        functools.partial(segment_kernel, shape, ahead),
        out_shape=(out, out),
        in_specs=[VMEM] * len(operands),
        out_specs=(VMEM, VMEM),
        scratch_shapes=[
            pltpu.VMEM((slot_count * blocks + SUB, LANES), jnp.float32),
            pltpu.VMEM((slot_count * blocks + 2 * SUB, LANES), jnp.float32),
            pltpu.VMEM((chunk + SUB, 2 * LANES), jnp.float32),
            pltpu.VMEM((chunk + SUB, 2 * LANES), jnp.float32),
            pltpu.VMEM((slot_count * blocks, LANES), jnp.float32),
            pltpu.VMEM((slot_count, 4 * blocks, 2 * LANES), jnp.bfloat16),
            pltpu.VMEM((2 * parts, block_rows, LANES), jnp.float32),
            pltpu.VMEM((stack_count + 1, blocks, LANES), jnp.float32),
            pltpu.VMEM((SUB, LANES), jnp.int32),
            pltpu.SMEM((SUB, LANES), jnp.int32),
            pltpu.SMEM((pair_count + UNROLL,), jnp.int32),
            pltpu.SemaphoreType.DMA((1,)),
        ],
        compiler_params=pltpu.CompilerParams(vmem_limit_bytes=KERNEL_BYTES),
        name="segment_stack",
    )(*on_chip(operands))


def local(records, row_dest, row_chan, row_len, templates, tmpl_chan, tmpl_off):
    slot_count, sample_count = records.shape
    size = lax.axis_size("tm")
    half = size // 2
    capacity = slot_count // size
    per_block, half_taps, taps = templates.shape
    lags = sample_count - taps - MAXOFF
    across = [(i, (i + half) % size) for i in range(size)]
    swap = [(0, 1), (1, 0)]
    shape = (half, capacity, sample_count // LANES, taps, per_block, half_taps, lags)

    def within(x, step):
        return lax.ppermute(
            x, "tm", [(i, (i // half) * half + ((i % half) ^ step)) for i in range(size)]
        )

    block, far_out, own_out = pack(
        records, row_dest, row_chan, row_len, templates, tmpl_chan, tmpl_off, half
    )

    far_rows = [far_out[0]] + [within(far_out[k], k) for k in range(1, half)]
    other = [
        lax.ppermute(block, "tm", [(i, (i ^ k) ^ half) for i in range(size)])
        for k in range(half)
    ]
    own_rows = [own_out[0]] + [within(own_out[k], k) for k in range(1, half)]
    keep, send = segment_stack(far_rows, far_rows, other, half, shape)
    far = keep + lax.ppermute(send, "chan", swap)
    far, *own_rows = lax.optimization_barrier((far, *own_rows))
    far = lax.ppermute(far, "tm", across)
    keep, send = segment_stack(own_rows, far_rows, other, 0, shape)
    total = keep + lax.ppermute(send, "chan", swap) + far
    return total[None]


def solution(mesh):
    in_specs = (
        P(("fam", "tm", "chan"), None),
        P(("fam", "tm", "chan")),
        P(("fam", "tm", "chan")),
        P(("fam", "tm", "chan")),
        P(("fam", "tm"), "chan", None),
        P(("fam", "tm"), "chan"),
        P(("fam", "tm"), "chan"),
    )
    out_specs = P(("fam", "tm"), None, None, "chan")
    return jax.shard_map(local, mesh=mesh, in_specs=in_specs, out_specs=out_specs, check_vma=False)
```

```python
import functools

import jax
import jax.numpy as jnp
from jax import lax
from jax.experimental import pallas as pl
from jax.experimental.pallas import tpu as pltpu
from jax.sharding import PartitionSpec as P


TCH = 16
MAXOFF = 256
STOPS = 4
LANES = 128
HALF = LANES // 2
SUB = 8
UNROLL = 16
PAIR_BITS = 8
SLOT_BITS = 6
PAIR_STEP = 1 << PAIR_BITS
SLOT_STEP = 1 << SLOT_BITS

FLOOR_SHARE = 0.25
TEMPLATE_EPS = 1e-06


SMEM = pl.BlockSpec(memory_space=pltpu.SMEM)
VMEM = pl.BlockSpec(memory_space=pltpu.VMEM)
KERNEL_BYTES = 24 << 20


def in_main(arrays):
    return [pltpu.with_memory_space_constraint(x, pltpu.HBM) for x in arrays]


def on_chip(arrays):
    return [pltpu.with_memory_space_constraint(x, pltpu.VMEM) for x in arrays]


def split(x):
    high = x.astype(jnp.bfloat16)
    return high, (x - high.astype(jnp.float32)).astype(jnp.bfloat16)


def pack_kernel(half, capacity, dest, chan, length, rec, templ, templ_chan, templ_off, *refs):
    block_out = refs[0]
    outs = refs[1 : 2 * half + 1]
    count, source, raw, rows, in_sems = refs[2 * half + 1 :]
    slot_count = dest.shape[0]
    blocks = rec.shape[1] // LANES
    me = lax.axis_index("tm")
    member, home = lax.rem(me, half), lax.div(me, half)
    pieces = in_sems.shape[0]
    piece_rows = slot_count // pieces
    arriving = []
    for p in range(pieces):
        part = pl.ds(p * piece_rows, piece_rows)
        arriving.append(pltpu.make_async_copy(rec.at[part], raw.at[part], in_sems.at[p]))
        arriving[-1].start()
    write_unit(templ, templ_chan, templ_off, block_out)

    def clear_count(i, c):
        count[i] = 0
        return c

    lax.fori_loop(0, count.shape[0], clear_count, 0)

    def clear_source(i, c):
        source[i] = -1
        return c

    lax.fori_loop(0, slot_count, clear_source, 0, unroll=8)

    def place(r, c):
        d = dest[r]
        used = d >= 0
        d = jnp.where(used, d, 2 * half)
        side = jnp.where(d >= half, 1, 0)
        step = jnp.bitwise_xor(d - side * half, member)
        rank = count[d]
        count[d] = rank + 1
        pos = (jnp.where(side == home, half, 0) + step) * capacity + rank
        source[jnp.where(used, pos, slot_count)] = r
        return c

    lax.fori_loop(0, slot_count, place, 0, unroll=8)

    def reform(g, c):
        first = pl.multiple_of(g * SUB, SUB)
        for b in range(blocks):
            rows[pl.ds(first * blocks + b, SUB, stride=blocks), :] = raw[
                pl.ds(first, SUB), b * LANES : (b + 1) * LANES
            ]
        return c

    for p in range(pieces):
        arriving[p].wait()
        lax.fori_loop(p * piece_rows // SUB, (p + 1) * piece_rows // SUB, reform, 0)
    flat = lax.broadcasted_iota(jnp.int32, (blocks, LANES), 0) * LANES + lax.broadcasted_iota(
        jnp.int32, (blocks, LANES), 1
    )
    last = blocks * LANES - 1
    for group, out in enumerate(outs):

        def emit(i, c, group=group, out=out):
            r = source[group * capacity + i]
            used = r >= 0
            row = jnp.maximum(r, 0)
            limit = jnp.where(used, length[row], 0)
            tag = jnp.where(used, chan[row], -1).astype(jnp.float32)
            tile = rows[pl.ds(pl.multiple_of(row * blocks, blocks), blocks), :]
            tile = jnp.where(flat < limit, tile, 0.0)
            out[i * blocks : (i + 1) * blocks, :] = jnp.where(flat == last, tag, tile)
            return c

        for i in range(capacity):
            emit(i, 0)
        if group < half:
            out[capacity * blocks :, :] = block_out[...]


def write_unit(templ, chan, off, out):
    per_block, half_taps, taps = templ.shape
    pair_rows = per_block * half_taps
    x = templ[...].reshape(pair_rows, taps)
    centred = x - jnp.mean(x, axis=-1, keepdims=True)
    energy = jnp.sum(centred * centred, axis=-1, keepdims=True)
    unit = centred / jnp.sqrt(energy + taps * TEMPLATE_EPS)
    high, rest = split(unit)
    middle, low = split(unit - high.astype(jnp.float32))
    del rest
    row_i = lax.broadcasted_iota(jnp.int32, (LANES, LANES), 0)
    lane_i = lax.broadcasted_iota(jnp.int32, (LANES, LANES), 1)
    turn = jnp.where(row_i == lax.rem(LANES - lane_i, LANES), 1.0, 0.0).astype(jnp.bfloat16)
    for j in range(taps // LANES):
        lanes = slice(j * LANES, (j + 1) * LANES)
        pieces = [
            jnp.dot(part[:, lanes], turn, preferred_element_type=jnp.float32)
            for part in (high, middle, low)
        ]
        out[j * pair_rows : (j + 1) * pair_rows, :] = pieces[0] + (pieces[1] + pieces[2])
    base = (taps // LANES) * pair_rows
    out[base:, :] = jnp.zeros((out.shape[0] - base, LANES), jnp.float32)
    row = jnp.zeros((1, LANES), jnp.float32)
    for which, ref in enumerate((chan, off)):
        for k in range(per_block):
            piece = ref[k : k + 1, :].astype(jnp.float32)
            first = which * pair_rows + k * half_taps
            row += jnp.pad(piece, ((0, 0), (first, LANES - first - half_taps)))
    out[base : base + 1, :] = row


def pack(records, row_dest, row_chan, row_len, templates, tmpl_chan, tmpl_off, half):
    slot_count, sample_count = records.shape
    capacity = slot_count // (2 * half)
    blocks = sample_count // LANES
    per_block, half_taps, taps = templates.shape
    block_rows = (taps // LANES) * per_block * half_taps + SUB
    pieces = 4 if slot_count % (4 * SUB) == 0 else 1
    far = pltpu.VMEM((capacity * blocks + block_rows, LANES), jnp.float32)
    own = pltpu.VMEM((capacity * blocks, LANES), jnp.float32)
    whole = pl.BlockSpec(memory_space=pl.ANY)
    block, *outs = pl.pallas_call(
        functools.partial(pack_kernel, half, capacity),
        out_shape=[pltpu.VMEM((block_rows, LANES), jnp.float32)]
        + [far] * half
        + [own] * half,
        in_specs=[SMEM] * 3 + [whole] + [VMEM] * 3,
        out_specs=[VMEM] * (2 * half + 1),
        scratch_shapes=[
            pltpu.SMEM((2 * half + 1,), jnp.int32),
            pltpu.SMEM((slot_count + 1,), jnp.int32),
            pltpu.VMEM((slot_count, sample_count), jnp.float32),
            pltpu.VMEM((slot_count * blocks, LANES), jnp.float32),
            pltpu.SemaphoreType.DMA((pieces,)),
        ],
        compiler_params=pltpu.CompilerParams(vmem_limit_bytes=KERNEL_BYTES),
        name="pack",
    )(*in_main((row_dest, row_chan, row_len, records, templates, tmpl_chan, tmpl_off)))
    return block, outs[:half], outs[half:]


def slots_at_once(slot_count):
    return next(n for n in (12, 8, 6, 4, 3, 2, 1) if slot_count % n == 0)


def window_kernel(shape, place, *refs):
    parts, capacity, blocks, taps = shape
    rows_in = refs[:parts]
    h_out, inv_out, tags_out, x_sc, y_sc, s_sc, q_sc = refs[-7:]
    slot_first = place * capacity
    slot_count = parts * capacity
    rows = slot_count * blocks
    stack_gain = (taps * TCH) ** 0.5 / TCH
    part_rows = capacity * blocks
    for k in range(parts):
        x_sc[k * part_rows : (k + 1) * part_rows, :] = rows_in[k][:part_rows, :]
    x_sc[rows:, :] = jnp.zeros((SUB, LANES), jnp.float32)
    tags_out[slot_first : slot_first + slot_count, :] = x_sc[
        pl.ds(blocks - 1, slot_count, stride=blocks), :
    ]

    row_i = lax.broadcasted_iota(jnp.int32, (LANES, LANES), 0)
    lane_i = lax.broadcasted_iota(jnp.int32, (LANES, LANES), 1)
    lower = row_i >= lane_i
    tail = lower.astype(jnp.float32).astype(jnp.bfloat16)
    ones = jnp.ones((LANES, LANES), jnp.bfloat16)
    sums = jnp.concatenate([tail, ones], axis=1)
    sums = jnp.concatenate([sums, sums], axis=0)
    chunk_slots = slots_at_once(slot_count)
    chunk = chunk_slots * blocks

    def prepare(g, c):
        base = pl.multiple_of(g * chunk, chunk)
        x0 = x_sc[pl.ds(base, chunk), :]
        high0, low0 = split(x0)
        s_sc[:chunk, :] = jnp.dot(
            jnp.concatenate([high0, low0], axis=1), sums, preferred_element_type=jnp.float32
        )
        square_high, square_low = split(x0 * x0)
        q_sc[:chunk, :] = jnp.dot(
            jnp.concatenate([square_high, square_low], axis=1),
            sums,
            preferred_element_type=jnp.float32,
        )

        def window(ref):
            return (
                ref[:chunk, :LANES]
                + ref[pl.ds(1, chunk), LANES:]
                + (ref[pl.ds(2, chunk), LANES:] - ref[pl.ds(2, chunk), :LANES])
            )

        win_sum = window(s_sc)
        variance = window(q_sc) - win_sum * win_sum / taps
        inv = stack_gain / jnp.sqrt(jnp.maximum(variance, FLOOR_SHARE * taps))
        inv_out[pl.ds(slot_first * blocks + base, chunk), :] = inv
        before = y_sc[pl.ds(base + SUB - 1, chunk), :]
        after = y_sc[pl.ds(base + SUB + 1, chunk), :]
        windows = (
            (jnp.where(left, x0, after), x_sc[pl.ds(base + 2, chunk), :]),
            (jnp.where(left, before, x0), after),
        )
        slot0 = slot_first + g * chunk_slots
        for i, window_pair in enumerate(windows):
            for j, part in enumerate(window_pair):
                lanes = slice(j * LANES, (j + 1) * LANES)
                for k, piece in enumerate(split(part)):
                    first = (2 * i + k) * blocks
                    h_out[pl.ds(slot0, chunk_slots), first : first + blocks, lanes] = piece.reshape(
                        chunk_slots, blocks, LANES
                    )
        return c

    s_sc[chunk:, :] = jnp.zeros((SUB, 2 * LANES), jnp.float32)
    q_sc[chunk:, :] = jnp.zeros((SUB, 2 * LANES), jnp.float32)
    left = lax.broadcasted_iota(jnp.int32, (chunk, LANES), 1) < HALF

    def turn(g, c):
        base = pl.multiple_of(g * chunk, chunk)
        y_sc[pl.ds(base + SUB, chunk), :] = pltpu.roll(x_sc[pl.ds(base, chunk), :], HALF, 1)
        return c

    y_sc[:SUB, :] = jnp.zeros((SUB, LANES), jnp.float32)
    y_sc[rows + SUB :, :] = jnp.zeros((SUB, LANES), jnp.float32)
    lax.fori_loop(0, slot_count // chunk_slots, turn, 0)
    lax.fori_loop(0, slot_count // chunk_slots, prepare, 0)


def row_windows(rows, shape, place, earlier):
    parts, capacity, blocks, _ = shape
    total = parts * capacity
    slot_count = len(rows) * capacity
    chunk = slots_at_once(slot_count) * blocks
    return pl.pallas_call(
        functools.partial(window_kernel, (len(rows),) + shape[1:], place),
        out_shape=(
            pltpu.VMEM((total, 4 * blocks, 2 * LANES), jnp.bfloat16),
            pltpu.VMEM((total * blocks, LANES), jnp.float32),
            pltpu.VMEM((total, LANES), jnp.float32),
        ),
        in_specs=[VMEM] * (len(rows) + len(earlier)),
        out_specs=(VMEM, VMEM, VMEM),
        input_output_aliases={len(rows) + i: i for i in range(len(earlier))},
        scratch_shapes=[
            pltpu.VMEM((slot_count * blocks + SUB, LANES), jnp.float32),
            pltpu.VMEM((slot_count * blocks + 2 * SUB, LANES), jnp.float32),
            pltpu.VMEM((chunk + SUB, 2 * LANES), jnp.float32),
            pltpu.VMEM((chunk + SUB, 2 * LANES), jnp.float32),
        ],
        compiler_params=pltpu.CompilerParams(vmem_limit_bytes=KERNEL_BYTES),
        name="row_windows",
    )(*on_chip((*rows, *earlier)))


def segment_kernel(shape, ahead, h_in, inv_in, tags_in, *refs):
    parts, capacity, blocks, _, per_block, half_taps, lags = shape
    near_in = refs[:parts]
    other_in = refs[parts : 2 * parts]
    keep, send, u_sc, acc, code_v, code_s, listed, sems = refs[2 * parts :]
    size = 2 * parts
    me = lax.axis_index("tm")
    core = lax.axis_index("chan")
    segment = lax.rem(me + ahead, size)
    member, home = lax.rem(me, parts), lax.div(me, parts)
    slot_count = parts * capacity
    pair_rows = per_block * half_taps
    pair_count = STOPS * pair_rows
    block_rows = u_sc.shape[1]
    part_rows = capacity * blocks
    for k in range(parts):
        index = jnp.bitwise_xor(member, k)
        u_sc[home * parts + index] = near_in[k][part_rows:, :]
        u_sc[(1 - home) * parts + index] = other_in[k][...]
    acc[...] = jnp.zeros_like(acc)

    lane_p = lax.broadcasted_iota(jnp.int32, (1, LANES), 1)
    chan_of = jnp.zeros((1, LANES), jnp.float32)
    off_of = jnp.zeros((1, LANES), jnp.float32)
    for s in range(STOPS):
        maps = u_sc[lax.rem(segment - s + size, size), block_rows - SUB : block_rows, :][:1]
        here = lax.div(lane_p, pair_rows) == s
        chan_of = jnp.where(here, pltpu.roll(maps, (s * pair_rows) % LANES, 1), chan_of)
        off_of = jnp.where(here, pltpu.roll(maps, ((s - 1) * pair_rows) % LANES, 1), off_of)
    tags = tags_in[:, LANES - 1 :]
    match = (tags == chan_of).astype(jnp.float32)
    slots = lax.broadcasted_iota(jnp.int32, (slot_count, LANES), 0).astype(jnp.float32)
    slot_of = jnp.sum(match * slots, axis=0, keepdims=True)
    held = jnp.sum(match, axis=0, keepdims=True)
    code = lane_p.astype(jnp.float32) + slot_of * PAIR_STEP + off_of * (PAIR_STEP * SLOT_STEP)
    code = jnp.where(held > 0, code, -1.0).astype(jnp.int32)
    code_v[...] = jnp.broadcast_to(code, (SUB, LANES))
    copy = pltpu.make_async_copy(code_v, code_s, sems.at[0])
    copy.start()

    copy.wait()

    def gather_pairs(i, filled):
        value = code_s[0, i]
        listed[filled] = value
        return filled + jnp.where(value >= 0, 1, 0)

    filled = lax.fori_loop(0, pair_count, gather_pairs, 0, unroll=16)
    groups = lax.div(filled + UNROLL - 1, UNROLL)
    for i in range(UNROLL):
        listed[filled + i] = pair_count

    lane_b = lax.broadcasted_iota(jnp.int32, (blocks, LANES), 1)
    row_h = lax.broadcasted_iota(jnp.int32, (HALF, LANES), 0)
    lane_h = lax.broadcasted_iota(jnp.int32, (HALF, LANES), 1)
    mask = (row_h >= lane_h).astype(jnp.float32).astype(jnp.bfloat16) > 0
    zero = jnp.zeros((HALF, LANES), jnp.bfloat16)
    left_b = lane_b < HALF

    def pairs(g, c):
        for j in range(UNROLL):
            value = listed[g * UNROLL + j]
            pair = jnp.bitwise_and(value, PAIR_STEP - 1)
            slot = jnp.bitwise_and(lax.shift_right_logical(value, PAIR_BITS), SLOT_STEP - 1)
            off = lax.shift_right_logical(value, PAIR_BITS + SLOT_BITS)
            stop = lax.div(pair, pair_rows)
            block = lax.rem(segment - stop + size, size)
            inner = pair - stop * pair_rows

            def circulant(row):
                return pltpu.roll(
                    jnp.broadcast_to(u_sc[block, pl.ds(row, 1), :], (HALF, LANES)),
                    0,
                    1,
                    stride=1,
                    stride_axis=0,
                )

            first = split(circulant(inner))
            second = split(circulant(inner + pair_rows))
            bands = [
                jnp.concatenate([jnp.where(mask, x, zero) for x in first], axis=1),
                jnp.concatenate([jnp.where(mask, y, x) for x, y in zip(first, second)], axis=1),
                jnp.concatenate([jnp.where(mask, zero, y) for y in second], axis=1),
            ]
            terms = jnp.dot(
                h_in[slot, :, : 3 * HALF],
                jnp.concatenate(bands, axis=0),
                preferred_element_type=jnp.float32,
            )
            front, back = (
                (part[:blocks, :LANES] + part[:blocks, LANES:])
                + (part[blocks:, :LANES] + part[blocks:, LANES:])
                for part in (terms[: 2 * blocks], terms[2 * blocks :])
            )
            back = jnp.where(left_b, pltpu.roll(back, blocks - 1, 0), back)
            corr = front + pltpu.roll(back, HALF, 1)
            ratio = corr * inv_in[pl.ds(pl.multiple_of(slot * blocks, blocks), blocks), :]
            by_lane = jnp.bitwise_and(off, LANES - 1)
            whole = off >= LANES
            here = pltpu.roll(ratio, lax.rem(LANES - by_lane, LANES), 1)
            after = pltpu.roll(here, blocks - 1, 0)
            beyond = pltpu.roll(here, blocks - 2, 0)
            moved = jnp.where(
                lane_b < LANES - by_lane,
                jnp.where(whole, after, here),
                jnp.where(whole, beyond, after),
            )
            acc[lax.div(pair, half_taps)] += moved
        return c

    lax.fori_loop(0, groups, pairs, 0)

    half_lags = lags // 2 // LANES
    for which, ref in ((core, keep), (1 - core, send)):
        for s in range(STOPS):
            stacks = slice(s * per_block, (s + 1) * per_block)
            for b in range(half_lags):
                ref[s, :, b * LANES : (b + 1) * LANES] = jnp.where(
                    which == 0, acc[stacks, b, :], acc[stacks, half_lags + b, :]
                )


def segment_stack(windows, near, other, ahead, shape):
    parts, _, blocks, _, per_block, half_taps, lags = shape
    stack_count = STOPS * per_block
    pair_count = stack_count * half_taps
    block_rows = other[0].shape[0]
    out = pltpu.VMEM((STOPS, per_block, lags // 2), jnp.float32)
    return pl.pallas_call(
        functools.partial(segment_kernel, shape, ahead),
        out_shape=(out, out),
        in_specs=[VMEM] * (2 * parts + 3),
        out_specs=(VMEM, VMEM),
        scratch_shapes=[
            pltpu.VMEM((2 * parts, block_rows, LANES), jnp.float32),
            pltpu.VMEM((stack_count + 1, blocks, LANES), jnp.float32),
            pltpu.VMEM((SUB, LANES), jnp.int32),
            pltpu.SMEM((SUB, LANES), jnp.int32),
            pltpu.SMEM((pair_count + UNROLL,), jnp.int32),
            pltpu.SemaphoreType.DMA((1,)),
        ],
        compiler_params=pltpu.CompilerParams(vmem_limit_bytes=KERNEL_BYTES),
        name="segment_stack",
    )(*on_chip((*windows, *near, *other)))


def local(records, row_dest, row_chan, row_len, templates, tmpl_chan, tmpl_off):
    slot_count, sample_count = records.shape
    size = lax.axis_size("tm")
    half = size // 2
    capacity = slot_count // size
    per_block, half_taps, taps = templates.shape
    lags = sample_count - taps - MAXOFF
    across = [(i, (i + half) % size) for i in range(size)]
    swap = [(0, 1), (1, 0)]
    shape = (half, capacity, sample_count // LANES, taps, per_block, half_taps, lags)

    def within(x, step):
        return lax.ppermute(
            x, "tm", [(i, (i // half) * half + ((i % half) ^ step)) for i in range(size)]
        )

    block, far_out, own_out = pack(
        records, row_dest, row_chan, row_len, templates, tmpl_chan, tmpl_off, half
    )

    far_rows, other, own_rows = [far_out[0]], [], [own_out[0]]
    for k in range(1, half):
        far_rows.append(within(far_out[k], k))
        own_rows.append(within(own_out[k], k))
    for k in range(half):
        other.append(
            lax.ppermute(block, "tm", [(i, (i ^ k) ^ half) for i in range(size)])
        )
    own_windows = row_windows(own_rows[:1], shape[:4], 0, ())
    windows = row_windows(far_rows[:-1], shape[:4], 0, ())
    windows = row_windows(far_rows[-1:], shape[:4], half - 1, windows)
    keep, send = segment_stack(windows, far_rows, other, half, shape)
    recv = lax.ppermute(send, "chan", swap)
    windows = row_windows(own_rows[1:-1], shape[:4], 1, own_windows)
    far = keep + recv
    far, *windows = lax.optimization_barrier((far, *windows))
    far = lax.ppermute(far, "tm", across)
    windows = row_windows(own_rows[-1:], shape[:4], half - 1, windows)
    keep, send = segment_stack(windows, far_rows, other, 0, shape)
    total = keep + lax.ppermute(send, "chan", swap) + far
    return total[None]


def solution(mesh):
    in_specs = (
        P(("fam", "tm", "chan"), None),
        P(("fam", "tm", "chan")),
        P(("fam", "tm", "chan")),
        P(("fam", "tm", "chan")),
        P(("fam", "tm"), "chan", None),
        P(("fam", "tm"), "chan"),
        P(("fam", "tm"), "chan"),
    )
    out_specs = P(("fam", "tm"), None, None, "chan")
    return jax.shard_map(local, mesh=mesh, in_specs=in_specs, out_specs=out_specs, check_vma=False)
```

```python
import functools

import jax
import jax.numpy as jnp
from jax import lax
from jax.experimental import pallas as pl
from jax.experimental.pallas import tpu as pltpu
from jax.sharding import PartitionSpec as P


TCH = 16
MAXOFF = 256
STOPS = 4
LANES = 128
HALF = LANES // 2
SUB = 8
UNROLL = 16
PAIR_BITS = 8
SLOT_BITS = 6
PAIR_STEP = 1 << PAIR_BITS
SLOT_STEP = 1 << SLOT_BITS

FLOOR_SHARE = 0.25
TEMPLATE_EPS = 1e-06


SMEM = pl.BlockSpec(memory_space=pltpu.SMEM)
VMEM = pl.BlockSpec(memory_space=pltpu.VMEM)
KERNEL_BYTES = 24 << 20


def in_main(arrays):
    return [pltpu.with_memory_space_constraint(x, pltpu.HBM) for x in arrays]


def on_chip(arrays):
    return [pltpu.with_memory_space_constraint(x, pltpu.VMEM) for x in arrays]


def split(x):
    high = x.astype(jnp.bfloat16)
    return high, (x - high.astype(jnp.float32)).astype(jnp.bfloat16)


def pack_kernel(half, capacity, dest, chan, length, rec, templ, templ_chan, templ_off, *refs):
    block_out = refs[0]
    outs = refs[1 : 2 * half + 1]
    count, source, raw, rows, in_sems = refs[2 * half + 1 :]
    slot_count = dest.shape[0]
    blocks = rec.shape[1] // LANES
    me = lax.axis_index("tm")
    member, home = lax.rem(me, half), lax.div(me, half)
    pieces = in_sems.shape[0]
    piece_rows = slot_count // pieces
    arriving = []
    for p in range(pieces):
        part = pl.ds(p * piece_rows, piece_rows)
        arriving.append(pltpu.make_async_copy(rec.at[part], raw.at[part], in_sems.at[p]))
        arriving[-1].start()
    write_unit(templ, templ_chan, templ_off, block_out)

    def clear_count(i, c):
        count[i] = 0
        return c

    lax.fori_loop(0, count.shape[0], clear_count, 0)

    def clear_source(i, c):
        source[i] = -1
        return c

    lax.fori_loop(0, slot_count, clear_source, 0, unroll=8)

    def place(r, c):
        d = dest[r]
        used = d >= 0
        d = jnp.where(used, d, 2 * half)
        side = jnp.where(d >= half, 1, 0)
        step = jnp.bitwise_xor(d - side * half, member)
        rank = count[d]
        count[d] = rank + 1
        pos = (jnp.where(side == home, half, 0) + step) * capacity + rank
        source[jnp.where(used, pos, slot_count)] = r
        return c

    lax.fori_loop(0, slot_count, place, 0, unroll=8)

    def reform(g, c):
        first = pl.multiple_of(g * SUB, SUB)
        for b in range(blocks):
            rows[pl.ds(first * blocks + b, SUB, stride=blocks), :] = raw[
                pl.ds(first, SUB), b * LANES : (b + 1) * LANES
            ]
        return c

    for p in range(pieces):
        arriving[p].wait()
        lax.fori_loop(p * piece_rows // SUB, (p + 1) * piece_rows // SUB, reform, 0)
    flat = lax.broadcasted_iota(jnp.int32, (blocks, LANES), 0) * LANES + lax.broadcasted_iota(
        jnp.int32, (blocks, LANES), 1
    )
    last = blocks * LANES - 1
    for group, out in enumerate(outs):

        def emit(i, c, group=group, out=out):
            r = source[group * capacity + i]
            used = r >= 0
            row = jnp.maximum(r, 0)
            limit = jnp.where(used, length[row], 0)
            tag = jnp.where(used, chan[row], -1).astype(jnp.float32)
            tile = rows[pl.ds(pl.multiple_of(row * blocks, blocks), blocks), :]
            tile = jnp.where(flat < limit, tile, 0.0)
            out[i * blocks : (i + 1) * blocks, :] = jnp.where(flat == last, tag, tile)
            return c

        for i in range(capacity):
            emit(i, 0)
        if group < half:
            out[capacity * blocks :, :] = block_out[...]


def write_unit(templ, chan, off, out):
    per_block, half_taps, taps = templ.shape
    pair_rows = per_block * half_taps
    x = templ[...].reshape(pair_rows, taps)
    centred = x - jnp.mean(x, axis=-1, keepdims=True)
    energy = jnp.sum(centred * centred, axis=-1, keepdims=True)
    unit = centred / jnp.sqrt(energy + taps * TEMPLATE_EPS)
    high, rest = split(unit)
    middle, low = split(unit - high.astype(jnp.float32))
    del rest
    row_i = lax.broadcasted_iota(jnp.int32, (LANES, LANES), 0)
    lane_i = lax.broadcasted_iota(jnp.int32, (LANES, LANES), 1)
    turn = jnp.where(row_i == lax.rem(LANES - lane_i, LANES), 1.0, 0.0).astype(jnp.bfloat16)
    for j in range(taps // LANES):
        lanes = slice(j * LANES, (j + 1) * LANES)
        pieces = [
            jnp.dot(part[:, lanes], turn, preferred_element_type=jnp.float32)
            for part in (high, middle, low)
        ]
        out[j * pair_rows : (j + 1) * pair_rows, :] = pieces[0] + (pieces[1] + pieces[2])
    base = (taps // LANES) * pair_rows
    out[base:, :] = jnp.zeros((out.shape[0] - base, LANES), jnp.float32)
    row = jnp.zeros((1, LANES), jnp.float32)
    for which, ref in enumerate((chan, off)):
        for k in range(per_block):
            piece = ref[k : k + 1, :].astype(jnp.float32)
            first = which * pair_rows + k * half_taps
            row += jnp.pad(piece, ((0, 0), (first, LANES - first - half_taps)))
    out[base : base + 1, :] = row


def pack(records, row_dest, row_chan, row_len, templates, tmpl_chan, tmpl_off, half):
    slot_count, sample_count = records.shape
    capacity = slot_count // (2 * half)
    blocks = sample_count // LANES
    per_block, half_taps, taps = templates.shape
    block_rows = (taps // LANES) * per_block * half_taps + SUB
    pieces = 4 if slot_count % (4 * SUB) == 0 else 1
    far = pltpu.VMEM((capacity * blocks + block_rows, LANES), jnp.float32)
    own = pltpu.VMEM((capacity * blocks, LANES), jnp.float32)
    whole = pl.BlockSpec(memory_space=pl.ANY)
    block, *outs = pl.pallas_call(
        functools.partial(pack_kernel, half, capacity),
        out_shape=[pltpu.VMEM((block_rows, LANES), jnp.float32)]
        + [far] * half
        + [own] * half,
        in_specs=[SMEM] * 3 + [whole] + [VMEM] * 3,
        out_specs=[VMEM] * (2 * half + 1),
        scratch_shapes=[
            pltpu.SMEM((2 * half + 1,), jnp.int32),
            pltpu.SMEM((slot_count + 1,), jnp.int32),
            pltpu.VMEM((slot_count, sample_count), jnp.float32),
            pltpu.VMEM((slot_count * blocks, LANES), jnp.float32),
            pltpu.SemaphoreType.DMA((pieces,)),
        ],
        compiler_params=pltpu.CompilerParams(vmem_limit_bytes=KERNEL_BYTES),
        name="pack",
    )(*in_main((row_dest, row_chan, row_len, records, templates, tmpl_chan, tmpl_off)))
    return block, outs[:half], outs[half:]


def slots_at_once(slot_count):
    return next(n for n in (12, 8, 6, 4, 3, 2, 1) if slot_count % n == 0)


def window_kernel(shape, place, *refs):
    parts, capacity, blocks, taps = shape
    rows_in = refs[:parts]
    h_out, inv_out, tags_out, x_sc, y_sc, s_sc, q_sc = refs[-7:]
    slot_first = place * capacity
    slot_count = parts * capacity
    rows = slot_count * blocks
    stack_gain = (taps * TCH) ** 0.5 / TCH
    part_rows = capacity * blocks
    for k in range(parts):
        x_sc[k * part_rows : (k + 1) * part_rows, :] = rows_in[k][:part_rows, :]
    x_sc[rows:, :] = jnp.zeros((SUB, LANES), jnp.float32)
    tags_out[slot_first : slot_first + slot_count, :] = x_sc[
        pl.ds(blocks - 1, slot_count, stride=blocks), :
    ]

    row_i = lax.broadcasted_iota(jnp.int32, (LANES, LANES), 0)
    lane_i = lax.broadcasted_iota(jnp.int32, (LANES, LANES), 1)
    lower = row_i >= lane_i
    tail = lower.astype(jnp.float32).astype(jnp.bfloat16)
    ones = jnp.ones((LANES, LANES), jnp.bfloat16)
    sums = jnp.concatenate([tail, ones], axis=1)
    sums = jnp.concatenate([sums, sums], axis=0)
    chunk_slots = slots_at_once(slot_count)
    chunk = chunk_slots * blocks

    def prepare(g, c):
        base = pl.multiple_of(g * chunk, chunk)
        x0 = x_sc[pl.ds(base, chunk), :]
        high0, low0 = split(x0)
        s_sc[:chunk, :] = jnp.dot(
            jnp.concatenate([high0, low0], axis=1), sums, preferred_element_type=jnp.float32
        )
        square_high, square_low = split(x0 * x0)
        q_sc[:chunk, :] = jnp.dot(
            jnp.concatenate([square_high, square_low], axis=1),
            sums,
            preferred_element_type=jnp.float32,
        )

        def window(ref):
            return (
                ref[:chunk, :LANES]
                + ref[pl.ds(1, chunk), LANES:]
                + (ref[pl.ds(2, chunk), LANES:] - ref[pl.ds(2, chunk), :LANES])
            )

        win_sum = window(s_sc)
        variance = window(q_sc) - win_sum * win_sum * (1.0 / taps)
        inv = stack_gain * lax.rsqrt(jnp.maximum(variance, FLOOR_SHARE * taps))
        inv_out[pl.ds(slot_first * blocks + base, chunk), :] = inv
        before = y_sc[pl.ds(base + SUB - 1, chunk), :]
        after = y_sc[pl.ds(base + SUB + 1, chunk), :]
        windows = (
            (jnp.where(left, x0, after), x_sc[pl.ds(base + 2, chunk), :]),
            (jnp.where(left, before, x0), after),
        )
        slot0 = slot_first + g * chunk_slots
        for i, window_pair in enumerate(windows):
            for j, part in enumerate(window_pair):
                lanes = slice(j * LANES, (j + 1) * LANES)
                for k, piece in enumerate(split(part)):
                    first = (2 * i + k) * blocks
                    h_out[pl.ds(slot0, chunk_slots), first : first + blocks, lanes] = piece.reshape(
                        chunk_slots, blocks, LANES
                    )
        return c

    s_sc[chunk:, :] = jnp.zeros((SUB, 2 * LANES), jnp.float32)
    q_sc[chunk:, :] = jnp.zeros((SUB, 2 * LANES), jnp.float32)
    left = lax.broadcasted_iota(jnp.int32, (chunk, LANES), 1) < HALF

    def turn(g, c):
        base = pl.multiple_of(g * chunk, chunk)
        y_sc[pl.ds(base + SUB, chunk), :] = pltpu.roll(x_sc[pl.ds(base, chunk), :], HALF, 1)
        return c

    y_sc[:SUB, :] = jnp.zeros((SUB, LANES), jnp.float32)
    y_sc[rows + SUB :, :] = jnp.zeros((SUB, LANES), jnp.float32)
    lax.fori_loop(0, slot_count // chunk_slots, turn, 0)
    lax.fori_loop(0, slot_count // chunk_slots, prepare, 0)


def row_windows(rows, shape, place, earlier):
    parts, capacity, blocks, _ = shape
    total = parts * capacity
    slot_count = len(rows) * capacity
    chunk = slots_at_once(slot_count) * blocks
    return pl.pallas_call(
        functools.partial(window_kernel, (len(rows),) + shape[1:], place),
        out_shape=(
            pltpu.VMEM((total, 4 * blocks, 2 * LANES), jnp.bfloat16),
            pltpu.VMEM((total * blocks, LANES), jnp.float32),
            pltpu.VMEM((total, LANES), jnp.float32),
        ),
        in_specs=[VMEM] * (len(rows) + len(earlier)),
        out_specs=(VMEM, VMEM, VMEM),
        input_output_aliases={len(rows) + i: i for i in range(len(earlier))},
        scratch_shapes=[
            pltpu.VMEM((slot_count * blocks + SUB, LANES), jnp.float32),
            pltpu.VMEM((slot_count * blocks + 2 * SUB, LANES), jnp.float32),
            pltpu.VMEM((chunk + SUB, 2 * LANES), jnp.float32),
            pltpu.VMEM((chunk + SUB, 2 * LANES), jnp.float32),
        ],
        compiler_params=pltpu.CompilerParams(vmem_limit_bytes=KERNEL_BYTES),
        name="row_windows",
    )(*on_chip((*rows, *earlier)))


def segment_kernel(shape, ahead, h_in, inv_in, tags_in, *refs):
    parts, capacity, blocks, _, per_block, half_taps, lags = shape
    near_in = refs[:parts]
    other_in = refs[parts : 2 * parts]
    keep, send, u_sc, acc, code_v, code_s, listed, sems = refs[2 * parts :]
    size = 2 * parts
    me = lax.axis_index("tm")
    core = lax.axis_index("chan")
    segment = lax.rem(me + ahead, size)
    member, home = lax.rem(me, parts), lax.div(me, parts)
    slot_count = parts * capacity
    pair_rows = per_block * half_taps
    pair_count = STOPS * pair_rows
    block_rows = u_sc.shape[1]
    part_rows = capacity * blocks
    for k in range(parts):
        index = jnp.bitwise_xor(member, k)
        u_sc[home * parts + index] = near_in[k][part_rows:, :]
        u_sc[(1 - home) * parts + index] = other_in[k][...]
    acc[...] = jnp.zeros_like(acc)

    lane_p = lax.broadcasted_iota(jnp.int32, (1, LANES), 1)
    chan_of = jnp.zeros((1, LANES), jnp.float32)
    off_of = jnp.zeros((1, LANES), jnp.float32)
    for s in range(STOPS):
        maps = u_sc[lax.rem(segment - s + size, size), block_rows - SUB : block_rows, :][:1]
        here = lax.div(lane_p, pair_rows) == s
        chan_of = jnp.where(here, pltpu.roll(maps, (s * pair_rows) % LANES, 1), chan_of)
        off_of = jnp.where(here, pltpu.roll(maps, ((s - 1) * pair_rows) % LANES, 1), off_of)
    tags = tags_in[:, LANES - 1 :]
    match = (tags == chan_of).astype(jnp.float32)
    slots = lax.broadcasted_iota(jnp.int32, (slot_count, LANES), 0).astype(jnp.float32)
    slot_of = jnp.sum(match * slots, axis=0, keepdims=True)
    held = jnp.sum(match, axis=0, keepdims=True)
    code = lane_p.astype(jnp.float32) + slot_of * PAIR_STEP + off_of * (PAIR_STEP * SLOT_STEP)
    code = jnp.where(held > 0, code, -1.0).astype(jnp.int32)
    code_v[...] = jnp.broadcast_to(code, (SUB, LANES))
    copy = pltpu.make_async_copy(code_v, code_s, sems.at[0])
    copy.start()

    copy.wait()

    def gather_pairs(i, filled):
        value = code_s[0, i]
        listed[filled] = value
        return filled + jnp.where(value >= 0, 1, 0)

    filled = lax.fori_loop(0, pair_count, gather_pairs, 0, unroll=16)
    groups = lax.div(filled + UNROLL - 1, UNROLL)
    for i in range(UNROLL):
        listed[filled + i] = pair_count

    lane_b = lax.broadcasted_iota(jnp.int32, (blocks, LANES), 1)
    row_h = lax.broadcasted_iota(jnp.int32, (HALF, LANES), 0)
    lane_h = lax.broadcasted_iota(jnp.int32, (HALF, LANES), 1)
    mask = (row_h >= lane_h).astype(jnp.float32).astype(jnp.bfloat16) > 0
    zero = jnp.zeros((HALF, LANES), jnp.bfloat16)
    left_b = lane_b < HALF

    def pairs(g, c):
        for j in range(UNROLL):
            value = listed[g * UNROLL + j]
            pair = jnp.bitwise_and(value, PAIR_STEP - 1)
            slot = jnp.bitwise_and(lax.shift_right_logical(value, PAIR_BITS), SLOT_STEP - 1)
            off = lax.shift_right_logical(value, PAIR_BITS + SLOT_BITS)
            stop = lax.div(pair, pair_rows)
            block = lax.rem(segment - stop + size, size)
            inner = pair - stop * pair_rows

            def circulant(row):
                return pltpu.roll(
                    jnp.broadcast_to(u_sc[block, pl.ds(row, 1), :], (HALF, LANES)),
                    0,
                    1,
                    stride=1,
                    stride_axis=0,
                )

            first = split(circulant(inner))
            second = split(circulant(inner + pair_rows))
            bands = [
                jnp.concatenate([jnp.where(mask, x, zero) for x in first], axis=1),
                jnp.concatenate([jnp.where(mask, y, x) for x, y in zip(first, second)], axis=1),
                jnp.concatenate([jnp.where(mask, zero, y) for y in second], axis=1),
            ]
            terms = jnp.dot(
                h_in[slot, :, : 3 * HALF],
                jnp.concatenate(bands, axis=0),
                preferred_element_type=jnp.float32,
            )
            front, back = (
                (part[:blocks, :LANES] + part[:blocks, LANES:])
                + (part[blocks:, :LANES] + part[blocks:, LANES:])
                for part in (terms[: 2 * blocks], terms[2 * blocks :])
            )
            back = jnp.where(left_b, pltpu.roll(back, blocks - 1, 0), back)
            corr = front + pltpu.roll(back, HALF, 1)
            ratio = corr * inv_in[pl.ds(pl.multiple_of(slot * blocks, blocks), blocks), :]
            by_lane = jnp.bitwise_and(off, LANES - 1)
            whole = off >= LANES
            here = pltpu.roll(ratio, lax.rem(LANES - by_lane, LANES), 1)
            after = pltpu.roll(here, blocks - 1, 0)
            beyond = pltpu.roll(here, blocks - 2, 0)
            moved = jnp.where(
                lane_b < LANES - by_lane,
                jnp.where(whole, after, here),
                jnp.where(whole, beyond, after),
            )
            acc[lax.div(pair, half_taps)] += moved
        return c

    lax.fori_loop(0, groups, pairs, 0)

    half_lags = lags // 2 // LANES
    for which, ref in ((core, keep), (1 - core, send)):
        for s in range(STOPS):
            stacks = slice(s * per_block, (s + 1) * per_block)
            for b in range(half_lags):
                ref[s, :, b * LANES : (b + 1) * LANES] = jnp.where(
                    which == 0, acc[stacks, b, :], acc[stacks, half_lags + b, :]
                )


def segment_stack(windows, near, other, ahead, shape):
    parts, _, blocks, _, per_block, half_taps, lags = shape
    stack_count = STOPS * per_block
    pair_count = stack_count * half_taps
    block_rows = other[0].shape[0]
    out = pltpu.VMEM((STOPS, per_block, lags // 2), jnp.float32)
    return pl.pallas_call(
        functools.partial(segment_kernel, shape, ahead),
        out_shape=(out, out),
        in_specs=[VMEM] * (2 * parts + 3),
        out_specs=(VMEM, VMEM),
        scratch_shapes=[
            pltpu.VMEM((2 * parts, block_rows, LANES), jnp.float32),
            pltpu.VMEM((stack_count + 1, blocks, LANES), jnp.float32),
            pltpu.VMEM((SUB, LANES), jnp.int32),
            pltpu.SMEM((SUB, LANES), jnp.int32),
            pltpu.SMEM((pair_count + UNROLL,), jnp.int32),
            pltpu.SemaphoreType.DMA((1,)),
        ],
        compiler_params=pltpu.CompilerParams(vmem_limit_bytes=KERNEL_BYTES),
        name="segment_stack",
    )(*on_chip((*windows, *near, *other)))


def local(records, row_dest, row_chan, row_len, templates, tmpl_chan, tmpl_off):
    slot_count, sample_count = records.shape
    size = lax.axis_size("tm")
    half = size // 2
    capacity = slot_count // size
    per_block, half_taps, taps = templates.shape
    lags = sample_count - taps - MAXOFF
    across = [(i, (i + half) % size) for i in range(size)]
    swap = [(0, 1), (1, 0)]
    shape = (half, capacity, sample_count // LANES, taps, per_block, half_taps, lags)

    def within(x, step):
        return lax.ppermute(
            x, "tm", [(i, (i // half) * half + ((i % half) ^ step)) for i in range(size)]
        )

    block, far_out, own_out = pack(
        records, row_dest, row_chan, row_len, templates, tmpl_chan, tmpl_off, half
    )

    far_rows, other, own_rows = [far_out[0]], [], [own_out[0]]
    for k in range(1, half):
        far_rows.append(within(far_out[k], k))
        own_rows.append(within(own_out[k], k))
    for k in range(half):
        other.append(
            lax.ppermute(block, "tm", [(i, (i ^ k) ^ half) for i in range(size)])
        )
    windows = row_windows(far_rows[:-1], shape[:4], 0, ())
    windows = row_windows(far_rows[-1:], shape[:4], half - 1, windows)
    keep, send = segment_stack(windows, far_rows, other, half, shape)
    recv = lax.ppermute(send, "chan", swap)
    windows = row_windows(own_rows[:-1], shape[:4], 0, ())
    far = keep + recv
    far, *windows = lax.optimization_barrier((far, *windows))
    far = lax.ppermute(far, "tm", across)
    windows = row_windows(own_rows[-1:], shape[:4], half - 1, windows)
    keep, send = segment_stack(windows, far_rows, other, 0, shape)
    total = keep + lax.ppermute(send, "chan", swap) + far
    return total[None]


def solution(mesh):
    in_specs = (
        P(("fam", "tm", "chan"), None),
        P(("fam", "tm", "chan")),
        P(("fam", "tm", "chan")),
        P(("fam", "tm", "chan")),
        P(("fam", "tm"), "chan", None),
        P(("fam", "tm"), "chan"),
        P(("fam", "tm"), "chan"),
    )
    out_specs = P(("fam", "tm"), None, None, "chan")
    return jax.shard_map(local, mesh=mesh, in_specs=in_specs, out_specs=out_specs, check_vma=False)
```
